512 devices in a mesh: prow: 16 (over y_hi, x, core), pcol: 32 (over y_lo, z).
Axes of the slice: x: 4, y: 4 (y_hi: 2, y_lo: 2; y = y_hi * 2 + y_lo), z: 16, core: 2. Of those that a mesh axis runs over, the one named last changes fastest.
Arguments:
- ancestor_inverse: float32 [8192, 8192], P('prow', 'pcol'), may hold values from -6 to 6
- block_mask: int32 [32, 32], replicated, may hold values 0 or 1
- block_ids: int32 [32], replicated, may hold values from 0 to 31, each once
- row_lists: int32 [4, 16], replicated, may hold values from 0 to 31, as said below
- panels: float32 [8192, 512], P(('prow', 'pcol')), may hold values from -0.109375 to 0.109375
- diag_inverse: float32 [4, 128, 128], replicated, may hold values from -6 to 6
Outputs:
- inverse_panels: float32 [8192, 512], P(('prow', 'pcol'))
- diag_blocks: float32 [4, 128, 128], replicated
The draws below stay inside these ranges and needn't reach their ends.
Inputs may be any that keep to these rules, and one draw needn't show every extreme that they name: `row_lists`: each row names 16 different ancestor blocks.
All inputs are finite; a program needn't handle non-finite values.
Results may differ from the reference program's by a relative error of at most 0.0003.
Values sent between devices are 32-bit elements; how exact they have to be, the bound alone decides.
No kernel may reach another device: no remote copies, remote signals or barrier semaphores. Data moves between devices by JAX's collectives and lax.ppermute only.
A program may use at most 64 MiB of HBM per device.

```python
import jax
import jax.numpy as jnp
from jax import lax

BLK = 256
W = 128
S = 4
NB = 32
ORDER = 8192
NR = 16


def draw_row_lists(key, part):
    supernode_keys = jax.random.split(jax.random.fold_in(key, 7), S)

    def choose(one_key):
        return jax.random.permutation(one_key, NB)[:NR].astype(jnp.int32)
    return jax.vmap(choose)(supernode_keys)


def with_ends(array, stream_key, low, largest):
    longest = array.shape.index(max(array.shape))
    spots = []
    for shift in (0, 1):
        where = [jax.random.randint(jax.random.fold_in(stream_key, axis), (), 0, length) for axis, length in enumerate(array.shape)]
        where[longest] = (where[longest] + shift) % array.shape[longest]
        spots.append(tuple(where))
    return array.at[spots[0]].set(low).at[spots[1]].set(largest)


def level_of(own_key, shape, shards, least, largest):
    gain = 1.0
    for dim, blocks in shards:
        heights = jax.random.uniform(jax.random.fold_in(jax.random.fold_in(own_key, 6), dim), (blocks,), jnp.float32, least / len(shards), largest / len(shards))
        gain = gain * jnp.repeat(jnp.exp(heights), shape[dim] // blocks).reshape((-1,) + (1,) * (len(shape) - 1 - dim))
    return gain


def gaussian(key, dims, width, limit, cuts=(), held_as=jnp.bfloat16):
    values = width * jax.random.normal(key, dims, jnp.float32)
    if cuts:
        values = values * level_of(key, dims, cuts, -0.22, 0.18)
    return jnp.clip(values, -limit, limit).astype(held_as)


def setup_inputs(seed: int = 0) -> dict:
    keys = jax.random.split(jax.random.key(seed), 7)
    ancestor_inverse = gaussian(keys[0], (ORDER, ORDER), 1.0, 6.0, ((0, 16), (1, 32)), jnp.float32)
    block_mask = with_ends((jax.random.randint(keys[1], (NB, NB), 0, 4) < 3).astype(jnp.int32), jax.random.fold_in(keys[1], 1), 0, 1)
    block_ids = jax.random.permutation(keys[2], NB).astype(jnp.int32)
    row_lists = draw_row_lists(jax.random.fold_in(keys[6], 71), 0)
    panels = gaussian(keys[4], (ORDER, S * W), (NR * BLK * 3 // 4) ** -0.5, 0.109375, ((0, 512),), jnp.float32)
    diag_inverse = gaussian(keys[5], (S, W, W), 1.0, 6.0, (), jnp.float32)
    return dict(ancestor_inverse=ancestor_inverse, block_mask=block_mask, block_ids=block_ids, row_lists=row_lists, panels=panels, diag_inverse=diag_inverse)


def reference(ancestor_inverse, block_mask, block_ids, row_lists, panels, diag_inverse):
    active_blocks = jnp.any(block_ids[:, None, None] == row_lists[None, :, :], axis=2).astype(jnp.float32)
    row_keep = jnp.repeat(jnp.repeat(active_blocks, BLK, axis=0), W, axis=1)
    active = panels * row_keep
    mask_f = block_mask.astype(jnp.float32)

    def one_block(block_index):
        block_rows = lax.dynamic_slice_in_dim(ancestor_inverse, (block_index * BLK).astype(jnp.int32), BLK, 0)
        keep_cols = jnp.repeat(mask_f[block_index], BLK)
        return jnp.dot(block_rows * keep_cols[None, :], active, precision=lax.Precision.HIGHEST, preferred_element_type=jnp.float32)

    summed = lax.map(one_block, jnp.arange(NB, dtype=jnp.int32)).reshape(NB * BLK, S * W)
    inverse_panels = -(row_keep * summed)
    diag_blocks = diag_inverse - jnp.einsum("isa,isb->sab", active.reshape(-1, S, W), inverse_panels.reshape(-1, S, W), precision=lax.Precision.HIGHEST)
    return inverse_panels, diag_blocks
```

```python
import jax
import jax.numpy as jnp
from jax import lax
from jax.sharding import Mesh
from jax.sharding import PartitionSpec as P

BLK = 256
W = 128
S = 4
ROW = ("yh", "x", "c")
COL = ("yl", "z")
PLANE = ("yh", "x", "c", "yl")
ALL = ("yh", "x", "c", "yl", "z")


def exchange(value, axis, groups=None):
    return lax.all_to_all(value, axis, 0, 0, tiled=True, axis_index_groups=groups)


def spread(value, axis, count):
    copies = jnp.broadcast_to(value[None], (count,) + value.shape)
    return lax.all_to_all(copies, axis, 0, 0, tiled=True)


def local(ancestor_inverse, block_mask, block_ids, row_lists, panels, diag_inverse):
    rows = lax.axis_size(ROW)
    cols = lax.axis_size(COL)
    depth = lax.axis_size("z")
    halves = lax.axis_size("yl")
    plane = rows * halves
    prow_index = lax.axis_index(ROW)
    pcol_index = lax.axis_index(COL)
    row_count, width = panels.shape
    block_total = block_ids.shape[0]
    row_span, col_span = ancestor_inverse.shape
    active_blocks = jnp.any(
        block_ids[:, None, None] == row_lists[None, :, :], axis=2
    ).astype(jnp.float32)
    own_block = (prow_index * cols + pcol_index) * row_count // BLK
    own_active = lax.dynamic_slice_in_dim(active_blocks, own_block, 1, 0)
    own_keep = jnp.repeat(own_active, W, axis=1)
    active_own = panels * own_keep

    chunks = col_span // row_count
    pairs = [(q * chunks + j, j * cols + q) for q in range(cols) for j in range(chunks)]
    moved = lax.ppermute(active_own, ALL, pairs)
    needed = spread(moved, ROW, rows).reshape(col_span, width)

    block_rows = row_span // BLK
    local_mask = lax.dynamic_slice(
        block_mask, (prow_index * block_rows, pcol_index), (block_rows, 1)
    ).astype(jnp.float32)
    masked = (ancestor_inverse.reshape(block_rows, BLK, col_span) * local_mask[:, :, None]).reshape(
        row_span, col_span
    )
    pair = 2
    deep = depth // pair
    masked = (
        masked.reshape(halves, deep, pair, row_count, col_span)
        .transpose(0, 2, 1, 3, 4)
        .reshape(row_span, col_span)
    )
    partial_value = jnp.dot(
        masked, needed, precision=lax.Precision.HIGHEST, preferred_element_type=jnp.float32
    )
    near = [
        [h * depth + z * pair + m for h in range(halves) for m in range(pair)] for z in range(deep)
    ]
    far = [[z * pair + m for z in range(deep)] for m in range(pair)]
    first = exchange(partial_value, COL, near)
    first = jnp.sum(first.reshape(halves * pair, deep * row_count, width), axis=0)
    second = exchange(first, "z", far)
    summed = jnp.sum(second.reshape(deep, row_count, width), axis=0)
    inverse_panels = -(own_keep * summed)

    local_diag = jnp.einsum(
        "isa,isb->sab",
        active_own.reshape(row_count, S, W),
        inverse_panels.reshape(row_count, S, W),
        precision=lax.Precision.HIGHEST,
    )
    part = S * W // plane
    terms = exchange(local_diag.reshape(S * W, W), PLANE)
    terms = jnp.sum(terms.reshape(plane, part, W), axis=0)
    terms = jnp.sum(spread(terms, "z", depth).reshape(depth, part, W), axis=0)
    diag_total = spread(terms, PLANE, plane).reshape(S, W, W)
    return (inverse_panels, diag_inverse - diag_total)


def solution(mesh):
    fine = Mesh(mesh.devices.reshape(2, 4, 2, 2, 16), ALL)
    placed = (P(ROW, COL), P(), P(), P(), P(ALL, None), P())
    return jax.shard_map(
        local,
        mesh=fine,
        in_specs=placed,
        out_specs=(P(ALL, None), P()),
        check_vma=False,
    )
```

```python
import jax
import jax.numpy as jnp
from jax import lax
from jax.sharding import Mesh
from jax.sharding import PartitionSpec as P


BLK = 256
W = 128
S = 4
SUB = 8
ROW = ("yh", "x", "c")
COL = ("yl", "zh", "zl")
NEAR = ("yl", "zl")
FAR = "zh"
WIDE = ("yh", "x", "c", "yl", "zl")
ALL = ("yh", "x", "c", "yl", "zh", "zl")


def exchange(value, axis):
    return lax.all_to_all(value, axis, 0, 0, tiled=True)


def spread(value, axis):
    copies = jnp.broadcast_to(value[None], (lax.axis_size(axis),) + value.shape)
    return lax.all_to_all(copies, axis, 0, 0, tiled=True)


def local(ancestor_inverse, block_mask, block_ids, row_lists, panels, diag_inverse):
    cols = lax.axis_size(COL)
    near = lax.axis_size(NEAR)
    far = lax.axis_size(FAR)
    wide = lax.axis_size(WIDE)
    halves = lax.axis_size("yl")
    pair = lax.axis_size("zl")
    prow_index = lax.axis_index(ROW)
    pcol_index = lax.axis_index(COL)
    row_count, width = panels.shape
    row_span, col_span = ancestor_inverse.shape
    active_blocks = jnp.any(
        block_ids[:, None, None] == row_lists[None, :, :], axis=2
    ).astype(jnp.float32)
    own_block = (prow_index * cols + pcol_index) * row_count // BLK
    own_active = lax.dynamic_slice_in_dim(active_blocks, own_block, 1, 0)
    own_keep = jnp.repeat(own_active, W, axis=1)
    active_own = panels * own_keep

    chunks = col_span // row_count
    pairs = [(q * chunks + j, j * cols + q) for q in range(cols) for j in range(chunks)]
    moved = lax.ppermute(active_own, ALL, pairs)
    active_far = spread(active_own, FAR).reshape(far * row_count, width)
    needed = spread(moved, ROW).reshape(col_span, width)

    block_rows = row_span // BLK
    local_mask = lax.dynamic_slice(
        block_mask, (prow_index * block_rows, pcol_index), (block_rows, 1)
    ).astype(jnp.float32)
    masked = (
        ancestor_inverse.reshape(block_rows, BLK, col_span) * local_mask[:, :, None]
    ).reshape(row_span, col_span)
    masked = (
        masked.reshape(halves, far, pair, row_count, col_span)
        .transpose(0, 2, 1, 3, 4)
        .reshape(row_span, col_span)
    )
    partial_value = jnp.dot(
        masked, needed, precision=lax.Precision.HIGHEST, preferred_element_type=jnp.float32
    )
    first = exchange(partial_value, NEAR)
    first = jnp.sum(first.reshape(near, far * row_count, width), axis=0)

    local_diag = jnp.einsum(
        "isa,isb->sab",
        active_far.reshape(far * row_count, S, W),
        first.reshape(far * row_count, S, W),
        precision=lax.Precision.HIGHEST,
    )
    part = S * W // wide
    terms = exchange(local_diag.reshape(S * W, W), WIDE)
    terms = jnp.sum(terms.reshape(wide, part, W), axis=0)
    tiles = row_count // SUB * S
    sent = first.reshape(far, row_count // SUB, SUB, S, W).transpose(0, 1, 3, 2, 4)
    sent = sent.reshape(far, tiles * SUB, W)
    copies = jnp.broadcast_to(terms[None], (far,) + terms.shape)
    both = exchange(jnp.concatenate([sent, copies], axis=1), FAR)
    both = jnp.sum(both, axis=0)
    summed = both[: tiles * SUB].reshape(row_count // SUB, S, SUB, W)
    summed = summed.transpose(0, 2, 1, 3).reshape(row_count, width)
    inverse_panels = -(own_keep * summed)
    terms = both[tiles * SUB :]
    diag_total = spread(terms, WIDE).reshape(S, W, W)
    return (inverse_panels, diag_inverse + diag_total)


def solution(mesh):
    fine = Mesh(mesh.devices.reshape(2, 4, 2, 2, 8, 2), ALL)
    placed = (P(ROW, COL), P(), P(), P(), P(ALL, None), P())
    return jax.shard_map(
        local,
        mesh=fine,
        in_specs=placed,
        out_specs=(P(ALL, None), P()),
        check_vma=False,
    )
```

```python
import jax
import jax.numpy as jnp
from jax import lax
from jax.sharding import Mesh
from jax.sharding import PartitionSpec as P


BLK = 256
W = 128
S = 4
ROW = ("yh", "x", "c")
COL = ("yl", "z")
PLANE = ("yh", "x", "c", "yl")
SIDE = ("yh", "x", "yl")
ALL = ("yh", "x", "c", "yl", "z")
SWAP = [(0, 1), (1, 0)]


def spread(value, axis):
    copies = jnp.broadcast_to(value[None], (lax.axis_size(axis),) + value.shape)
    return lax.all_to_all(copies, axis, 0, 0, tiled=True)


def body(ancestor_inverse, block_mask, block_ids, row_lists, panels, diag_inverse):
    cols = lax.axis_size(COL)
    deep = lax.axis_size("z")
    prow_index = lax.axis_index(ROW)
    pcol_index = lax.axis_index(COL)
    core = lax.axis_index("c")
    side = lax.axis_index("yl")
    row_count, width = panels.shape
    half = width // 2
    row_span, col_span = ancestor_inverse.shape
    active_blocks = jnp.any(
        block_ids[:, None, None] == row_lists[None, :, :], axis=2
    ).astype(jnp.float32)
    own_block = (prow_index * cols + pcol_index) * row_count // BLK
    own_active = lax.dynamic_slice_in_dim(active_blocks, own_block, 1, 0)
    own_keep = jnp.repeat(own_active, W, axis=1)
    active_own = panels * own_keep

    chunks = col_span // row_count
    plane = lax.axis_size(PLANE)
    pairs = [
        (q * chunks + j, (q // deep * chunks + j) * deep + q % deep)
        for q in range(cols)
        for j in range(chunks)
    ]
    moved = lax.ppermute(active_own, ALL, pairs)

    by_core = active_own.reshape(row_count, 2, half).transpose(1, 0, 2)
    mine = jnp.where(core == 0, by_core[0], by_core[1])
    theirs = jnp.where(core == 0, by_core[1], by_core[0])
    active_pair = jnp.stack([mine, lax.ppermute(theirs, "c", SWAP)])

    block_rows = row_span // BLK
    local_mask = lax.dynamic_slice(
        block_mask, (prow_index * block_rows, pcol_index), (block_rows, 1)
    ).astype(jnp.float32)
    masked = ancestor_inverse.reshape(block_rows, BLK, col_span) * local_mask[:, :, None]
    kept = jnp.where(side == 0, masked[0], masked[1])
    sent = jnp.where(side == 0, masked[1], masked[0])
    came = lax.ppermute(sent, "yl", SWAP)
    own_rows = jnp.where(
        side == 0,
        jnp.concatenate([kept, came], axis=1),
        jnp.concatenate([came, kept], axis=1),
    )
    other_rows = lax.ppermute(own_rows, "c", SWAP)
    both_rows = jnp.stack(
        [
            own_rows.reshape(deep, row_count, 2 * col_span),
            other_rows.reshape(deep, row_count, 2 * col_span),
        ],
        axis=1,
    ).reshape(row_span, 2 * col_span)

    halves = moved.reshape(row_count, 2, half).transpose(1, 0, 2)
    shape = tuple(lax.axis_size(name) for name in PLANE)
    outgoing = jnp.broadcast_to(
        halves[None, None, :, None], shape + (row_count, half)
    ).reshape(plane, row_count, half)
    needed = lax.all_to_all(outgoing, PLANE, 0, 0, tiled=True).reshape(2 * col_span, half)

    partial_value = jnp.dot(
        both_rows, needed, precision=lax.Precision.HIGHEST, preferred_element_type=jnp.float32
    ).reshape(deep, 2 * row_count, half)
    parts = lax.all_to_all(partial_value, "z", 0, 0, tiled=True)
    summed = jnp.sum(parts, axis=0).reshape(2, row_count, half)

    back = lax.ppermute(summed[1], "c", SWAP)
    full = jnp.where(
        core == 0,
        jnp.concatenate([summed[0], back], axis=1),
        jnp.concatenate([back, summed[0]], axis=1),
    )
    inverse_panels = -(own_keep * full)

    local_diag = jnp.einsum(
        "isa,isb->sab",
        active_pair.reshape(2 * row_count, S // 2, W),
        summed.reshape(2 * row_count, S // 2, W),
        precision=lax.Precision.HIGHEST,
    )
    peers = lax.axis_size(SIDE)
    part = S // 2 * W // peers
    terms = lax.all_to_all(local_diag.reshape(peers, part, W), SIDE, 0, 0, tiled=True)
    terms = jnp.sum(terms, axis=0)
    terms = jnp.sum(spread(terms, "z"), axis=0)
    diag_total = spread(terms, PLANE).reshape(shape + (part, W))
    diag_total = diag_total.transpose(2, 0, 1, 3, 4, 5).reshape(S, W, W)
    return (inverse_panels, diag_inverse + diag_total)


def solution(mesh):
    fine = Mesh(mesh.devices.reshape(2, 4, 2, 2, 16), ALL)
    placed = (P(ROW, COL), P(), P(), P(), P(ALL, None), P())
    return jax.shard_map(
        body,
        mesh=fine,
        in_specs=placed,
        out_specs=(P(ALL, None), P()),
        check_vma=False,
    )
```

```python
import jax
import jax.numpy as jnp
from jax import lax
from jax.sharding import Mesh
from jax.sharding import PartitionSpec as P


BLK = 256
W = 128
S = 4
ROW = ("yh", "x", "c")
COL = ("yl", "zh", "zl")
DEPTH = ("zh", "zl")
PLANE = ("yh", "x", "c", "yl")
SIDE = ("yh", "x", "yl")
BACK = ("c", "yh", "x", "yl")
ALL = ("yh", "x", "c", "yl", "zh", "zl")
SWAP = [(0, 1), (1, 0)]


def spread(value, axis):
    copies = jnp.broadcast_to(value[None], (lax.axis_size(axis),) + value.shape)
    return lax.all_to_all(copies, axis, 0, 0, tiled=True)


def body(ancestor_inverse, block_mask, block_ids, row_lists, panels, diag_inverse):
    cols = lax.axis_size(COL)
    deep = lax.axis_size(DEPTH)
    far = lax.axis_size("zh")
    near = lax.axis_size("zl")
    prow_index = lax.axis_index(ROW)
    pcol_index = lax.axis_index(COL)
    core = lax.axis_index("c")
    side = lax.axis_index("yl")
    odd = lax.axis_index("zl")
    row_count, width = panels.shape
    half = width // 2
    row_span, col_span = ancestor_inverse.shape
    active_blocks = jnp.any(
        block_ids[:, None, None] == row_lists[None, :, :], axis=2
    ).astype(jnp.float32)
    own_block = (prow_index * cols + pcol_index) * row_count // BLK
    own_active = lax.dynamic_slice_in_dim(active_blocks, own_block, 1, 0)
    own_keep = jnp.repeat(own_active, W, axis=1)
    active_own = panels * own_keep

    chunks = col_span // row_count
    plane = lax.axis_size(PLANE)
    pairs = [
        (q * chunks + j, (q // deep * chunks + j) * deep + q % deep)
        for q in range(cols)
        for j in range(chunks)
    ]
    moved = lax.ppermute(active_own, ALL, pairs)

    by_core = active_own.reshape(row_count, 2, half).transpose(1, 0, 2)
    mine = jnp.where(core == 0, by_core[0], by_core[1])
    theirs = jnp.where(core == 0, by_core[1], by_core[0])
    active_pair = jnp.stack([mine, lax.ppermute(theirs, "c", SWAP)])

    block_rows = row_span // BLK
    blocks = ancestor_inverse.reshape(block_rows, BLK, col_span)
    kept = jnp.where(side == 0, blocks[0], blocks[1])
    sent = jnp.where(side == 0, blocks[1], blocks[0])
    came = lax.ppermute(sent, "yl", SWAP)
    own_rows = jnp.where(
        side == 0,
        jnp.concatenate([kept, came], axis=1),
        jnp.concatenate([came, kept], axis=1),
    )
    other_rows = lax.ppermute(own_rows, "c", SWAP)

    def keep_cols(grid_row):
        marks = lax.dynamic_slice(block_mask, (grid_row * block_rows + side, 0), (1, cols))
        marks = marks.reshape(cols // deep, deep)
        marks = lax.dynamic_slice(marks, (0, lax.axis_index(DEPTH)), (cols // deep, 1))
        return jnp.repeat(marks.reshape(cols // deep).astype(jnp.float32), col_span)

    def by_depth(rows, grid_row):
        rows = rows * keep_cols(grid_row)[None, :]
        return rows.reshape(far, near, row_count, 2 * col_span)

    pieces = jnp.stack(
        [by_depth(own_rows, prow_index), by_depth(other_rows, prow_index ^ 1)], axis=2
    )
    leave = jnp.where(odd == 0, pieces[:, 1], pieces[:, 0]).reshape(-1, 2 * col_span)
    stay = jnp.where(odd == 0, pieces[:, 0], pieces[:, 1]).reshape(-1, 2 * col_span)

    halves = moved.reshape(row_count, 2, half).transpose(1, 0, 2)
    shape = tuple(lax.axis_size(name) for name in PLANE)
    outgoing = jnp.broadcast_to(
        halves[None, None, :, None], shape + (row_count, half)
    ).reshape(plane, row_count, half)
    needed = lax.all_to_all(outgoing, PLANE, 0, 0, tiled=True).reshape(2 * col_span, half)

    def product(rows):
        value = jnp.dot(
            rows, needed, precision=lax.Precision.HIGHEST, preferred_element_type=jnp.float32
        )
        return value.reshape(far, 2 * row_count, half)

    leaving = product(leave)
    arrived = lax.ppermute(leaving, "zl", SWAP)
    pair_sum = product(stay) + arrived
    parts = lax.all_to_all(pair_sum, "zh", 0, 0, tiled=True)
    summed = jnp.sum(parts, axis=0).reshape(2, row_count, half)

    back = lax.ppermute(summed[1], "c", SWAP)
    full = jnp.where(
        core == 0,
        jnp.concatenate([summed[0], back], axis=1),
        jnp.concatenate([back, summed[0]], axis=1),
    )
    inverse_panels = -(own_keep * full)

    local_diag = jnp.einsum(
        "isa,isb->sab",
        active_pair.reshape(2 * row_count, S // 2, W),
        summed.reshape(2 * row_count, S // 2, W),
        precision=lax.Precision.HIGHEST,
    )
    peers = lax.axis_size(SIDE)
    part = S // 2 * W // peers
    terms = lax.all_to_all(local_diag.reshape(peers, part, W), SIDE, 0, 0, tiled=True)
    terms = jnp.sum(terms, axis=0)
    terms = jnp.sum(spread(terms, DEPTH), axis=0)
    own_part = lax.axis_index(BACK) * part
    terms = lax.dynamic_slice_in_dim(diag_inverse.reshape(S * W, W), own_part, part, 0) + terms
    diag_blocks = spread(terms, BACK).reshape(S, W, W)
    return (inverse_panels, diag_blocks)


def solution(mesh):
    fine = Mesh(mesh.devices.reshape(2, 4, 2, 2, 8, 2), ALL)
    placed = (P(ROW, COL), P(), P(), P(), P(ALL, None), P())
    return jax.shard_map(
        body,
        mesh=fine,
        in_specs=placed,
        out_specs=(P(ALL, None), P()),
        check_vma=False,
    )
```

```python
import jax
import jax.numpy as jnp
from jax import lax
from jax.sharding import Mesh
from jax.sharding import PartitionSpec as P


BLK = 256
W = 128
S = 4
YH, XS, CS, YL, ZH, ZL = 2, 4, 2, 2, 8, 2
ROW = ("yh", "x", "c")
COL = ("yl", "zh", "zl")
SIDE = ("yh", "x", "zl")
BACK = ("c", "yl", "yh", "x", "zl")
ALL = ("yh", "x", "c", "yl", "zh", "zl")
SWAP = [(0, 1), (1, 0)]


def flat_of(yh, x, c, yl, zh, zl):
    return ((((yh * XS + x) * CS + c) * YL + yl) * ZH + zh) * ZL + zl


def place_of(flat):
    out = []
    for size in (ZL, ZH, YL, CS, XS, YH):
        out.append(flat % size)
        flat //= size
    return tuple(reversed(out))


def hops(one, two):
    total = 0
    for a, b, size in (
        (one[1], two[1], XS),
        (one[0] * YL + one[3], two[0] * YL + two[3], YH * YL),
        (one[4] * ZL + one[5], two[4] * ZL + two[5], ZH * ZL),
    ):
        gap = abs(a - b) % size
        total += min(gap, size - gap)
    return total


def assign(sources, targets):
    near = [[hops(place_of(s), place_of(t)) for t in targets] for s in sources]
    owner = {}

    def place(s, limit, seen):
        for t in sorted(range(len(targets)), key=lambda t: near[s][t]):
            if near[s][t] > limit or t in seen:
                continue
            seen.add(t)
            if t not in owner or place(owner[t], limit, seen):
                owner[t] = s
                return True
        return False

    limit = 0
    for s in range(len(sources)):
        while not place(s, limit, set()):
            limit += 1
    return {sources[s]: targets[t] for t, s in owner.items()}


def routes(chunks):
    pairs, groups = [], []
    for zh in range(ZH):
        blocks = [(h * ZH + zh) * ZL + zl for h in range(YL) for zl in range(ZL)]
        where = {}
        for k in range(S):
            sources = [q * chunks + j for q in blocks for j in range(k, chunks, S)]
            targets = [
                flat_of(yh, x, k // YL, k % YL, zh, zl)
                for yh in range(YH)
                for x in range(XS)
                for zl in range(ZL)
            ]
            where.update(assign(sources, targets))
        order = [where[q * chunks + j] for q in blocks for j in range(chunks)]
        pairs += [(q * chunks + j, where[q * chunks + j]) for q in blocks for j in range(chunks)]
        groups.append(order)
    return pairs, groups


def spread(value, axis):
    copies = jnp.broadcast_to(value[None], (lax.axis_size(axis),) + value.shape)
    return lax.all_to_all(copies, axis, 0, 0, tiled=True)


def pick(index, one, two):
    return jnp.where(index == 0, one, two)


def in_order(index, own, other, axis):
    return pick(
        index,
        jnp.concatenate([own, other], axis=axis),
        jnp.concatenate([other, own], axis=axis),
    )


def body(ancestor_inverse, block_mask, block_ids, row_lists, panels, diag_inverse):
    cols = lax.axis_size(COL)
    prow_index = lax.axis_index(ROW)
    pcol_index = lax.axis_index(COL)
    core, side, odd = lax.axis_index("c"), lax.axis_index("yl"), lax.axis_index("zl")
    mine = core * YL + side
    row_count, _ = panels.shape
    row_span, col_span = ancestor_inverse.shape
    chunks = col_span // row_count
    pairs, groups = routes(chunks)
    active_blocks = jnp.any(
        block_ids[:, None, None] == row_lists[None, :, :], axis=2
    ).astype(jnp.float32)
    own_block = (prow_index * cols + pcol_index) * row_count // BLK
    own_active = lax.dynamic_slice_in_dim(active_blocks, own_block, 1, 0)
    own_keep = jnp.repeat(own_active, W, axis=1)
    active_own = panels * own_keep

    moved = lax.ppermute(active_own, ALL, pairs)

    blocks = ancestor_inverse.reshape(YL, ZH, ZL, row_count, col_span)
    kept = pick(odd, blocks[:, :, 0], blocks[:, :, 1]).reshape(-1, col_span)
    sent = pick(odd, blocks[:, :, 1], blocks[:, :, 0]).reshape(-1, col_span)
    came = lax.ppermute(sent, "zl", SWAP)
    two = in_order(odd, kept, came, 1)
    across = lax.ppermute(two, "yl", SWAP)
    four = in_order(side, two, across, 1)
    other = lax.ppermute(four, "c", SWAP)

    def masked(rows, grid_row):
        marks = lax.dynamic_slice(block_mask, (grid_row * YL, 0), (YL, cols)).reshape(YL, YL, ZH, ZL)
        marks = lax.dynamic_slice(
            marks, (0, 0, lax.axis_index("zh"), 0), (YL, YL, 1, ZL)
        ).reshape(YL, YL * ZL)
        marks = jnp.repeat(marks.astype(jnp.float32), col_span, axis=1)
        return rows.reshape(YL, ZH, row_count, -1) * marks[:, None, None, :]

    rows = jnp.stack([masked(four, prow_index), masked(other, prow_index ^ 1)])
    rows = rows.transpose(2, 0, 1, 3, 4).reshape(row_span, YL * ZL * col_span)

    by_node = moved.reshape(row_count, S, W).transpose(1, 0, 2)
    outgoing = jnp.broadcast_to(by_node[None], (chunks, S, row_count, W))
    outgoing = outgoing.reshape(chunks * S, row_count, W)
    needed = lax.all_to_all(outgoing, ALL, 0, 0, tiled=True, axis_index_groups=groups)
    partial_value = jnp.dot(
        rows,
        needed.reshape(-1, W),
        precision=lax.Precision.HIGHEST,
        preferred_element_type=jnp.float32,
    ).reshape(ZH, CS * YL * row_count, W)
    parts = lax.all_to_all(partial_value, "zh", 0, 0, tiled=True)
    summed = jnp.sum(parts, axis=0).reshape(CS, YL, row_count, W)

    shifts = ((0, 1), (1, 0), (1, 1))
    swaps = [
        [(m, m ^ (dc * YL + dy)) for m in range(CS * YL)] for dc, dy in shifts
    ]
    own_nodes = active_own.reshape(row_count, S, W)

    def node(index):
        return lax.dynamic_slice_in_dim(own_nodes, index, 1, 1)[:, 0]

    a01, a10, a11 = [
        lax.ppermute(node(mine ^ (dc * YL + dy)), ("c", "yl"), swap)
        for (dc, dy), swap in zip(shifts, swaps)
    ]
    a00 = node(mine)
    active_group = jnp.concatenate(
        [pick(side, a00, a01), pick(side, a01, a00), pick(side, a10, a11), pick(side, a11, a10)]
    )
    local_diag = jnp.dot(
        active_group.T, summed.reshape(-1, W), precision=lax.Precision.HIGHEST
    )
    peers = lax.axis_size(SIDE)
    part = W // peers
    terms = lax.all_to_all(local_diag.reshape(peers, part, W), SIDE, 0, 0, tiled=True)
    terms = jnp.sum(terms, axis=0)
    terms = jnp.sum(spread(terms, "zh"), axis=0)
    own_part = lax.axis_index(BACK) * part
    terms = lax.dynamic_slice_in_dim(diag_inverse.reshape(S * W, W), own_part, part, 0) + terms
    diag_blocks = spread(terms, BACK).reshape(S, W, W)

    r00 = pick(side, summed[0, 0], summed[0, 1])
    r01, r10, r11 = [
        lax.ppermute(pick(side ^ dy, summed[dc, 0], summed[dc, 1]), ("c", "yl"), swap)
        for (dc, dy), swap in zip(shifts, swaps)
    ]
    columns = []
    for k in range(S):
        which = mine ^ k
        columns.append(
            jnp.where(which < 2, jnp.where(which == 0, r00, r01), jnp.where(which == 2, r10, r11))
        )
    inverse_panels = -(own_keep * jnp.concatenate(columns, axis=1))
    return (inverse_panels, diag_blocks)


def solution(mesh):
    fine = Mesh(mesh.devices.reshape(YH, XS, CS, YL, ZH, ZL), ALL)
    placed = (P(ROW, COL), P(), P(), P(), P(ALL, None), P())
    return jax.shard_map(
        body,
        mesh=fine,
        in_specs=placed,
        out_specs=(P(ALL, None), P()),
        check_vma=False,
    )
```

```python
import jax
import jax.numpy as jnp
from jax import lax
from jax.sharding import Mesh
from jax.sharding import PartitionSpec as P


BLK = 256
W = 128
S = 4
YH, XS, CS, YL, ZH, ZL = 2, 4, 2, 2, 8, 2
ROW = ("yh", "x", "c")
COL = ("yl", "zh", "zl")
SIDE = ("yh", "x", "zl")
BACK = ("c", "yl", "yh", "x", "zl")
ALL = ("yh", "x", "c", "yl", "zh", "zl")
SWAP = [(0, 1), (1, 0)]


def flat_of(yh, x, c, yl, zh, zl):
    return ((((yh * XS + x) * CS + c) * YL + yl) * ZH + zh) * ZL + zl


def place_of(flat):
    out = []
    for size in (ZL, ZH, YL, CS, XS, YH):
        out.append(flat % size)
        flat //= size
    return tuple(reversed(out))


def hops(one, two):
    total = 0
    for a, b, size in (
        (one[1], two[1], XS),
        (one[0] * YL + one[3], two[0] * YL + two[3], YH * YL),
        (one[4] * ZL + one[5], two[4] * ZL + two[5], ZH * ZL),
    ):
        gap = abs(a - b) % size
        total += min(gap, size - gap)
    return total


def assign(sources, targets):
    near = [[hops(place_of(s), place_of(t)) for t in targets] for s in sources]
    owner = {}

    def place(s, limit, seen):
        for t in sorted(range(len(targets)), key=lambda t: near[s][t]):
            if near[s][t] > limit or t in seen:
                continue
            seen.add(t)
            if t not in owner or place(owner[t], limit, seen):
                owner[t] = s
                return True
        return False

    limit = 0
    for s in range(len(sources)):
        while not place(s, limit, set()):
            limit += 1
    return {sources[s]: targets[t] for t, s in owner.items()}


def routes(chunks):
    pairs, groups = [], []
    for zh in range(ZH):
        blocks = [(h * ZH + zh) * ZL + zl for h in range(YL) for zl in range(ZL)]
        where = {}
        for k in range(S):
            sources = [q * chunks + j for q in blocks for j in range(k, chunks, S)]
            targets = [
                flat_of(yh, x, k // YL, k % YL, zh, zl)
                for yh in range(YH)
                for x in range(XS)
                for zl in range(ZL)
            ]
            where.update(assign(sources, targets))
        order = [where[q * chunks + j] for q in blocks for j in range(chunks)]
        pairs += [(q * chunks + j, where[q * chunks + j]) for q in blocks for j in range(chunks)]
        groups.append(order)
    return pairs, groups


def spread(value, axis):
    copies = jnp.broadcast_to(value[None], (lax.axis_size(axis),) + value.shape)
    return lax.all_to_all(copies, axis, 0, 0, tiled=True)


def pick(index, one, two):
    return jnp.where(index == 0, one, two)


def in_order(index, own, other, axis):
    return pick(
        index,
        jnp.concatenate([own, other], axis=axis),
        jnp.concatenate([other, own], axis=axis),
    )


def body(ancestor_inverse, block_mask, block_ids, row_lists, panels, diag_inverse):
    cols = lax.axis_size(COL)
    prow_index = lax.axis_index(ROW)
    pcol_index = lax.axis_index(COL)
    core, side, odd = lax.axis_index("c"), lax.axis_index("yl"), lax.axis_index("zl")
    row_count, width = panels.shape
    row_span, col_span = ancestor_inverse.shape
    chunks = col_span // row_count
    pairs, groups = routes(chunks)
    active_blocks = jnp.any(
        block_ids[:, None, None] == row_lists[None, :, :], axis=2
    ).astype(jnp.float32)
    own_block = (prow_index * cols + pcol_index) * row_count // BLK
    own_active = lax.dynamic_slice_in_dim(active_blocks, own_block, 1, 0)
    own_keep = jnp.repeat(own_active, W, axis=1)
    active_own = panels * own_keep

    moved = lax.ppermute(active_own, ALL, pairs)

    own_nodes = active_own.reshape(row_count, S, W).transpose(1, 0, 2)
    copies = jnp.broadcast_to(own_nodes[:, None], (S, ZH, row_count, W))
    active_group = lax.all_to_all(
        copies.reshape(S * ZH, row_count, W), ("c", "yl", "zh"), 0, 0, tiled=True
    )

    blocks = ancestor_inverse.reshape(YL, ZH, ZL, row_count, col_span)
    kept = pick(odd, blocks[:, :, 0], blocks[:, :, 1]).reshape(-1, col_span)
    sent = pick(odd, blocks[:, :, 1], blocks[:, :, 0]).reshape(-1, col_span)
    came = lax.ppermute(sent, "zl", SWAP)
    two = in_order(odd, kept, came, 1)
    across = lax.ppermute(two, "yl", SWAP)
    four = in_order(side, two, across, 1)
    other = lax.ppermute(four, "c", SWAP)

    def masked(rows, grid_row):
        marks = lax.dynamic_slice(block_mask, (grid_row * YL, 0), (YL, cols)).reshape(YL, YL, ZH, ZL)
        marks = lax.dynamic_slice(
            marks, (0, 0, lax.axis_index("zh"), 0), (YL, YL, 1, ZL)
        ).reshape(YL, YL * ZL)
        marks = jnp.repeat(marks.astype(jnp.float32), col_span, axis=1)
        return rows.reshape(YL, ZH, row_count, -1) * marks[:, None, None, :]

    rows = in_order(core, masked(four, prow_index)[None], masked(other, prow_index ^ 1)[None], 0)
    rows = rows.transpose(2, 0, 1, 3, 4).reshape(row_span, YL * ZL * col_span)

    by_node = moved.reshape(row_count, S, W).transpose(1, 0, 2)
    outgoing = jnp.broadcast_to(by_node[None], (chunks, S, row_count, W))
    outgoing = outgoing.reshape(chunks * S, row_count, W)
    needed = lax.all_to_all(outgoing, ALL, 0, 0, tiled=True, axis_index_groups=groups)
    partial_value = jnp.dot(
        rows,
        needed.reshape(-1, W),
        precision=lax.Precision.HIGHEST,
        preferred_element_type=jnp.float32,
    ).reshape(ZH, CS * YL, row_count, W)
    local_diag = lax.dot_general(
        active_group.reshape(-1, W),
        partial_value.transpose(1, 0, 2, 3).reshape(-1, W),
        (((0,), (0,)), ((), ())),
        precision=lax.Precision.HIGHEST,
    )
    peers = lax.axis_size(SIDE)
    part = W // peers
    terms = lax.all_to_all(local_diag.reshape(peers, part, W), SIDE, 0, 0, tiled=True)
    terms = jnp.sum(terms, axis=0)
    members = CS * YL
    copies = jnp.broadcast_to(terms[None], (ZH, part, W))
    both = jnp.concatenate(
        [partial_value.reshape(ZH, members * row_count, W), copies], axis=1
    )
    both = jnp.sum(lax.all_to_all(both, "zh", 0, 0, tiled=True), axis=0)
    summed = both[: members * row_count].reshape(CS, YL, row_count, W)
    own_part = lax.axis_index(BACK) * part
    own_diag = lax.dynamic_slice_in_dim(diag_inverse.reshape(S * W, W), own_part, part, 0)
    diag_blocks = spread(own_diag + both[members * row_count :], BACK).reshape(S, W, W)

    from_core = lax.ppermute(pick(core, summed[1], summed[0]), "c", SWAP)
    held = in_order(core, pick(core, summed[0], summed[1])[None], from_core[None], 0)
    from_side = lax.ppermute(pick(side, held[:, 1], held[:, 0]), "yl", SWAP)
    nodes = in_order(side, pick(side, held[:, 0], held[:, 1])[:, None], from_side[:, None], 1)
    full = nodes.reshape(S, row_count, W).transpose(1, 0, 2).reshape(row_count, width)
    inverse_panels = -(own_keep * full)
    return (inverse_panels, diag_blocks)


def solution(mesh):
    fine = Mesh(mesh.devices.reshape(YH, XS, CS, YL, ZH, ZL), ALL)
    placed = (P(ROW, COL), P(), P(), P(), P(ALL, None), P())
    return jax.shard_map(
        body,
        mesh=fine,
        in_specs=placed,
        out_specs=(P(ALL, None), P()),
        check_vma=False,
    )
```

```python
import jax
import jax.numpy as jnp
from jax import lax
from jax.sharding import Mesh
from jax.sharding import PartitionSpec as P


BLK = 256
W = 128
S = 4
YH, XS, CS, YL, ZH, ZL = 2, 4, 2, 2, 8, 2
ROW = ("yh", "x", "c")
COL = ("yl", "zh", "zl")
DEPTH = ("zh", "zl")
SIDE = ("yh", "x", "yl", "zl")
BACK = ("c", "yh", "x", "yl", "zl")
ALL = ("yh", "x", "c", "yl", "zh", "zl")
SWAP = [(0, 1), (1, 0)]


def flat_of(yh, x, c, yl, zh, zl):
    return ((((yh * XS + x) * CS + c) * YL + yl) * ZH + zh) * ZL + zl


def place_of(flat):
    out = []
    for size in (ZL, ZH, YL, CS, XS, YH):
        out.append(flat % size)
        flat //= size
    return tuple(reversed(out))


def hops(one, two):
    total = 0
    for a, b, size in (
        (one[1], two[1], XS),
        (one[0] * YL + one[3], two[0] * YL + two[3], YH * YL),
        (one[4] * ZL + one[5], two[4] * ZL + two[5], ZH * ZL),
    ):
        gap = abs(a - b) % size
        total += min(gap, size - gap)
    return total


def assign(sources, targets):
    near = [[hops(place_of(s), place_of(t)) for t in targets] for s in sources]
    owner = {}

    def place(s, limit, seen):
        for t in sorted(range(len(targets)), key=lambda t: near[s][t]):
            if near[s][t] > limit or t in seen:
                continue
            seen.add(t)
            if t not in owner or place(owner[t], limit, seen):
                owner[t] = s
                return True
        return False

    limit = 0
    for s in range(len(sources)):
        while not place(s, limit, set()):
            limit += 1
    return {sources[s]: targets[t] for t, s in owner.items()}


def routes(chunks):
    pairs, groups = [], []
    for z in range(ZH * ZL):
        blocks = [h * ZH * ZL + z for h in range(YL)]
        where = {}
        for c in range(CS):
            sources = [q * chunks + j for q in blocks for j in range(c, chunks, CS)]
            targets = [
                flat_of(yh, x, c, yl, z // ZL, z % ZL)
                for yh in range(YH)
                for x in range(XS)
                for yl in range(YL)
            ]
            where.update(assign(sources, targets))
        order = [q * chunks + j for q in blocks for j in range(chunks)]
        pairs += [(source, where[source]) for source in order]
        groups.append([where[source] for source in order])
    return pairs, groups


def spread(value, axis):
    copies = jnp.broadcast_to(value[None], (lax.axis_size(axis),) + value.shape)
    return lax.all_to_all(copies, axis, 0, 0, tiled=True)


def body(ancestor_inverse, block_mask, block_ids, row_lists, panels, diag_inverse):
    cols = lax.axis_size(COL)
    deep = lax.axis_size(DEPTH)
    far = lax.axis_size("zh")
    near = lax.axis_size("zl")
    prow_index = lax.axis_index(ROW)
    pcol_index = lax.axis_index(COL)
    core = lax.axis_index("c")
    side = lax.axis_index("yl")
    odd = lax.axis_index("zl")
    row_count, width = panels.shape
    half = width // 2
    row_span, col_span = ancestor_inverse.shape
    active_blocks = jnp.any(
        block_ids[:, None, None] == row_lists[None, :, :], axis=2
    ).astype(jnp.float32)
    own_block = (prow_index * cols + pcol_index) * row_count // BLK
    own_active = lax.dynamic_slice_in_dim(active_blocks, own_block, 1, 0)
    own_keep = jnp.repeat(own_active, W, axis=1)
    active_own = panels * own_keep

    chunks = col_span // row_count
    pairs, groups = routes(chunks)
    moved = lax.ppermute(active_own, ALL, pairs)

    by_core = active_own.reshape(row_count, 2, half).transpose(1, 0, 2)
    mine = jnp.where(core == 0, by_core[0], by_core[1])
    theirs = jnp.where(core == 0, by_core[1], by_core[0])
    active_pair = jnp.stack([mine, lax.ppermute(theirs, "c", SWAP)])

    block_rows = row_span // BLK
    blocks = ancestor_inverse.reshape(block_rows, BLK, col_span)
    kept = jnp.where(side == 0, blocks[0], blocks[1])
    sent = jnp.where(side == 0, blocks[1], blocks[0])
    came = lax.ppermute(sent, "yl", SWAP)
    own_rows = jnp.where(
        side == 0,
        jnp.concatenate([kept, came], axis=1),
        jnp.concatenate([came, kept], axis=1),
    )
    other_rows = lax.ppermute(own_rows, "c", SWAP)

    def keep_cols(grid_row):
        marks = lax.dynamic_slice(block_mask, (grid_row * block_rows + side, 0), (1, cols))
        marks = marks.reshape(cols // deep, deep)
        marks = lax.dynamic_slice(marks, (0, lax.axis_index(DEPTH)), (cols // deep, 1))
        return jnp.repeat(marks.reshape(cols // deep).astype(jnp.float32), col_span)

    def by_depth(rows, grid_row):
        rows = rows * keep_cols(grid_row)[None, :]
        return rows.reshape(far, near, row_count, 2 * col_span)

    pieces = jnp.stack(
        [by_depth(own_rows, prow_index), by_depth(other_rows, prow_index ^ 1)], axis=2
    )
    leave = jnp.where(odd == 0, pieces[:, 1], pieces[:, 0]).reshape(-1, 2 * col_span)
    stay = jnp.where(odd == 0, pieces[:, 0], pieces[:, 1]).reshape(-1, 2 * col_span)

    halves = moved.reshape(row_count, CS, half).transpose(1, 0, 2)
    outgoing = jnp.broadcast_to(halves[None], (chunks * YL // CS, CS, row_count, half))
    outgoing = outgoing.reshape(chunks * YL, row_count, half)
    needed = lax.all_to_all(
        outgoing, ALL, 0, 0, tiled=True, axis_index_groups=groups
    ).reshape(2 * col_span, half)

    def product(rows):
        value = jnp.dot(
            rows, needed, precision=lax.Precision.HIGHEST, preferred_element_type=jnp.float32
        )
        return value.reshape(far, 2 * row_count, half)

    leaving = product(leave)
    arrived = lax.ppermute(leaving, "zl", SWAP)
    pair_sum = product(stay) + arrived
    part = S // 2 * W // lax.axis_size(SIDE)
    own_diag = lax.dynamic_slice_in_dim(
        diag_inverse.reshape(S * W, W), lax.axis_index(BACK) * part, part, 0
    )
    pair_sum, own_diag = lax.optimization_barrier((pair_sum, own_diag))
    parts = lax.all_to_all(pair_sum, "zh", 0, 0, tiled=True)
    summed = jnp.sum(parts, axis=0).reshape(2, row_count, half)

    back = lax.ppermute(summed[1], "c", SWAP)
    full = jnp.where(
        core == 0,
        jnp.concatenate([summed[0], back], axis=1),
        jnp.concatenate([back, summed[0]], axis=1),
    )
    inverse_panels = -(own_keep * full)

    local_diag = jnp.einsum(
        "isa,isb->sab",
        active_pair.reshape(2 * row_count, S // 2, W),
        summed.reshape(2 * row_count, S // 2, W),
        precision=lax.Precision.HIGHEST,
    )
    peers = lax.axis_size(SIDE)
    terms = lax.all_to_all(local_diag.reshape(peers, part, W), SIDE, 0, 0, tiled=True)
    terms = jnp.sum(terms, axis=0)
    terms = own_diag + jnp.sum(spread(terms, "zh"), axis=0)
    diag_blocks = spread(terms, BACK).reshape(S, W, W)
    return (inverse_panels, diag_blocks)


def solution(mesh):
    fine = Mesh(mesh.devices.reshape(YH, XS, CS, YL, ZH, ZL), ALL)
    placed = (P(ROW, COL), P(), P(), P(), P(ALL, None), P())
    return jax.shard_map(
        body,
        mesh=fine,
        in_specs=placed,
        out_specs=(P(ALL, None), P()),
        check_vma=False,
    )
```

```python
import jax
import jax.numpy as jnp
from jax import lax
from jax.sharding import Mesh
from jax.sharding import PartitionSpec as P


BLK = 256
W = 128
S = 4
YH, XS, CS, YL, ZH, ZL = 2, 4, 2, 2, 8, 2
ROW = ("yh", "x", "c")
COL = ("yl", "zh", "zl")
DEPTH = ("zh", "zl")
SIDE = ("yh", "x", "yl", "zl")
BACK = ("c", "yh", "x", "yl", "zl")
ALL = ("yh", "x", "c", "yl", "zh", "zl")
SWAP = [(0, 1), (1, 0)]


def flat_of(yh, x, c, yl, zh, zl):
    return ((((yh * XS + x) * CS + c) * YL + yl) * ZH + zh) * ZL + zl


def place_of(flat):
    out = []
    for size in (ZL, ZH, YL, CS, XS, YH):
        out.append(flat % size)
        flat //= size
    return tuple(reversed(out))


def hops(one, two):
    total = 0
    for a, b, size in (
        (one[1], two[1], XS),
        (one[0] * YL + one[3], two[0] * YL + two[3], YH * YL),
        (one[4] * ZL + one[5], two[4] * ZL + two[5], ZH * ZL),
    ):
        gap = abs(a - b) % size
        total += min(gap, size - gap)
    return total


def assign(sources, targets):
    near = [[hops(place_of(s), place_of(t)) for t in targets] for s in sources]
    owner = {}

    def place(s, limit, seen):
        for t in sorted(range(len(targets)), key=lambda t: near[s][t]):
            if near[s][t] > limit or t in seen:
                continue
            seen.add(t)
            if t not in owner or place(owner[t], limit, seen):
                owner[t] = s
                return True
        return False

    limit = 0
    for s in range(len(sources)):
        while not place(s, limit, set()):
            limit += 1
    return {sources[s]: targets[t] for t, s in owner.items()}


def routes(chunks):
    pairs, groups = [], []
    for z in range(ZH * ZL):
        blocks = [h * ZH * ZL + z for h in range(YL)]
        where = {}
        for c in range(CS):
            sources = [q * chunks + j for q in blocks for j in range(c, chunks, CS)]
            targets = [
                flat_of(yh, x, c, yl, z // ZL, z % ZL)
                for yh in range(YH)
                for x in range(XS)
                for yl in range(YL)
            ]
            where.update(assign(sources, targets))
        order = [q * chunks + j for q in blocks for j in range(chunks)]
        pairs += [(source, where[source]) for source in order]
        groups.append([where[source] for source in order])
    return pairs, groups


def spread(value, axis):
    copies = jnp.broadcast_to(value[None], (lax.axis_size(axis),) + value.shape)
    return lax.all_to_all(copies, axis, 0, 0, tiled=True)


def body(ancestor_inverse, block_mask, block_ids, row_lists, panels, diag_inverse):
    cols = lax.axis_size(COL)
    deep = lax.axis_size(DEPTH)
    far = lax.axis_size("zh")
    near = lax.axis_size("zl")
    prow_index = lax.axis_index(ROW)
    pcol_index = lax.axis_index(COL)
    core = lax.axis_index("c")
    side = lax.axis_index("yl")
    odd = lax.axis_index("zl")
    row_count, width = panels.shape
    half = width // 2
    row_span, col_span = ancestor_inverse.shape
    active_blocks = jnp.any(
        block_ids[:, None, None] == row_lists[None, :, :], axis=2
    ).astype(jnp.float32)
    own_block = (prow_index * cols + pcol_index) * row_count // BLK
    own_active = lax.dynamic_slice_in_dim(active_blocks, own_block, 1, 0)
    own_keep = jnp.repeat(own_active, W, axis=1)
    active_own = panels * own_keep

    chunks = col_span // row_count
    pairs, groups = routes(chunks)
    moved = lax.ppermute(panels, ALL, pairs)

    moved, active_own = lax.optimization_barrier((moved, active_own))

    by_core = active_own.reshape(row_count, 2, half).transpose(1, 0, 2)
    mine = jnp.where(core == 0, by_core[0], by_core[1])
    theirs = jnp.where(core == 0, by_core[1], by_core[0])
    active_pair = jnp.stack([mine, lax.ppermute(theirs, "c", SWAP)])

    block_rows = row_span // BLK
    blocks = ancestor_inverse.reshape(block_rows, BLK, col_span)
    kept = jnp.where(side == 0, blocks[0], blocks[1])
    sent = jnp.where(side == 0, blocks[1], blocks[0])
    came = lax.ppermute(sent, "yl", SWAP)
    own_rows = jnp.where(
        side == 0,
        jnp.concatenate([kept, came], axis=1),
        jnp.concatenate([came, kept], axis=1),
    )
    other_rows = lax.ppermute(own_rows, "c", SWAP)

    def keep_cols(grid_row):
        marks = lax.dynamic_slice(block_mask, (grid_row * block_rows + side, 0), (1, cols))
        marks = marks.reshape(cols // deep, deep)
        marks = lax.dynamic_slice(marks, (0, lax.axis_index(DEPTH)), (cols // deep, 1))
        return jnp.repeat(marks.reshape(cols // deep).astype(jnp.float32), col_span)

    def by_depth(rows, grid_row):
        rows = rows * keep_cols(grid_row)[None, :]
        return rows.reshape(far, near, row_count, 2 * col_span)

    pieces = jnp.stack(
        [by_depth(own_rows, prow_index), by_depth(other_rows, prow_index ^ 1)], axis=2
    )
    leave = jnp.where(odd == 0, pieces[:, 1], pieces[:, 0]).reshape(-1, 2 * col_span)
    stay = jnp.where(odd == 0, pieces[:, 0], pieces[:, 1]).reshape(-1, 2 * col_span)

    blocks_at = [0] * len(pairs)
    for source, target in pairs:
        blocks_at[target] = source // chunks
    held = jnp.asarray(blocks_at, jnp.int32)[prow_index * cols + pcol_index]
    held_keep = jnp.repeat(lax.dynamic_slice_in_dim(active_blocks, held, 1, 0), W, axis=1)
    halves = (moved * held_keep).reshape(row_count, CS, half).transpose(1, 0, 2)
    outgoing = jnp.broadcast_to(halves[None], (chunks * YL // CS, CS, row_count, half))
    outgoing = outgoing.reshape(chunks * YL, row_count, half)
    needed = lax.all_to_all(
        outgoing, ALL, 0, 0, tiled=True, axis_index_groups=groups
    ).reshape(2 * col_span, half)

    def product(rows):
        value = jnp.dot(
            rows, needed, precision=lax.Precision.HIGHEST, preferred_element_type=jnp.float32
        )
        return value.reshape(far, 2 * row_count, half)

    leaving = product(leave)
    arrived = lax.ppermute(leaving, "zl", SWAP)
    staying = product(stay)
    staying, arrived = lax.optimization_barrier((staying, arrived))
    pair_sum = staying + arrived
    part = S // 2 * W // lax.axis_size(SIDE)
    own_diag = lax.dynamic_slice_in_dim(
        diag_inverse.reshape(S * W, W), lax.axis_index(BACK) * part, part, 0
    )
    pair_sum, own_diag = lax.optimization_barrier((pair_sum, own_diag))
    parts = lax.all_to_all(pair_sum, "zh", 0, 0, tiled=True)
    summed = jnp.sum(parts, axis=0).reshape(2, row_count, half)

    back = lax.ppermute(summed[1], "c", SWAP)
    full = jnp.where(
        core == 0,
        jnp.concatenate([summed[0], back], axis=1),
        jnp.concatenate([back, summed[0]], axis=1),
    )
    inverse_panels = -(own_keep * full)

    local_diag = jnp.einsum(
        "isa,isb->sab",
        active_pair.reshape(2 * row_count, S // 2, W),
        summed.reshape(2 * row_count, S // 2, W),
        precision=lax.Precision.HIGHEST,
    )
    peers = lax.axis_size(SIDE)
    terms = lax.all_to_all(local_diag.reshape(peers, part, W), SIDE, 0, 0, tiled=True)
    terms = jnp.sum(terms, axis=0)
    terms = own_diag + jnp.sum(spread(terms, "zh"), axis=0)
    diag_blocks = spread(terms, BACK).reshape(S, W, W)
    return (inverse_panels, diag_blocks)


def solution(mesh):
    fine = Mesh(mesh.devices.reshape(YH, XS, CS, YL, ZH, ZL), ALL)
    placed = (P(ROW, COL), P(), P(), P(), P(ALL, None), P())
    return jax.shard_map(
        body,
        mesh=fine,
        in_specs=placed,
        out_specs=(P(ALL, None), P()),
        check_vma=False,
    )
```

```python
import jax
import jax.numpy as jnp
from jax import lax
from jax.sharding import Mesh
from jax.sharding import PartitionSpec as P


BLK = 256
W = 128
S = 4
YH, XS, CS, YL, ZH, ZL = 2, 4, 2, 2, 8, 2
ROW = ("yh", "x", "c")
COL = ("yl", "zh", "zl")
DEPTH = ("zh", "zl")
SIDE = ("yh", "x", "yl", "zl")
BACK = ("c", "yh", "x", "yl", "zl")
ALL = ("yh", "x", "c", "yl", "zh", "zl")
SWAP = [(0, 1), (1, 0)]


def flat_of(yh, x, c, yl, zh, zl):
    return ((((yh * XS + x) * CS + c) * YL + yl) * ZH + zh) * ZL + zl


def place_of(flat):
    out = []
    for size in (ZL, ZH, YL, CS, XS, YH):
        out.append(flat % size)
        flat //= size
    return tuple(reversed(out))


def hops(one, two):
    total = 0
    for a, b, size in (
        (one[1], two[1], XS),
        (one[0] * YL + one[3], two[0] * YL + two[3], YH * YL),
        (one[4] * ZL + one[5], two[4] * ZL + two[5], ZH * ZL),
    ):
        gap = abs(a - b) % size
        total += min(gap, size - gap)
    return total


def assign(sources, targets):
    near = [[hops(place_of(s), place_of(t)) for t in targets] for s in sources]
    owner = {}

    def place(s, limit, seen):
        for t in sorted(range(len(targets)), key=lambda t: near[s][t]):
            if near[s][t] > limit or t in seen:
                continue
            seen.add(t)
            if t not in owner or place(owner[t], limit, seen):
                owner[t] = s
                return True
        return False

    limit = 0
    for s in range(len(sources)):
        while not place(s, limit, set()):
            limit += 1
    return {sources[s]: targets[t] for t, s in owner.items()}


def routes(chunks):
    pairs, groups = [], []
    for z in range(ZH * ZL):
        blocks = [h * ZH * ZL + z for h in range(YL)]
        where = {}
        for c in range(CS):
            sources = [q * chunks + j for q in blocks for j in range(c, chunks, CS)]
            targets = [
                flat_of(yh, x, c, yl, z // ZL, z % ZL)
                for yh in range(YH)
                for x in range(XS)
                for yl in range(YL)
            ]
            where.update(assign(sources, targets))
        order = [q * chunks + j for q in blocks for j in range(chunks)]
        pairs += [(source, where[source]) for source in order]
        groups.append([where[source] for source in order])
    return pairs, groups


def spread(value, axis):
    copies = jnp.broadcast_to(value[None], (lax.axis_size(axis),) + value.shape)
    return lax.all_to_all(copies, axis, 0, 0, tiled=True)


def body(ancestor_inverse, block_mask, block_ids, row_lists, panels, diag_inverse):
    cols = lax.axis_size(COL)
    deep = lax.axis_size(DEPTH)
    far = lax.axis_size("zh")
    near = lax.axis_size("zl")
    prow_index = lax.axis_index(ROW)
    pcol_index = lax.axis_index(COL)
    core = lax.axis_index("c")
    side = lax.axis_index("yl")
    odd = lax.axis_index("zl")
    row_count, width = panels.shape
    half = width // 2
    row_span, col_span = ancestor_inverse.shape
    active_blocks = jnp.any(
        block_ids[:, None, None] == row_lists[None, :, :], axis=2
    ).astype(jnp.float32)
    own_block = (prow_index * cols + pcol_index) * row_count // BLK
    own_active = lax.dynamic_slice_in_dim(active_blocks, own_block, 1, 0)
    own_keep = jnp.repeat(own_active, W, axis=1)
    active_own = panels * own_keep

    chunks = col_span // row_count
    pairs, groups = routes(chunks)

    moved = lax.ppermute(panels, ALL, pairs)

    block_rows = row_span // BLK
    blocks = ancestor_inverse.reshape(block_rows, BLK, col_span)
    kept = jnp.where(side == 0, blocks[0], blocks[1])
    sent = jnp.where(side == 0, blocks[1], blocks[0])
    came = lax.ppermute(sent, "yl", SWAP)
    own_rows = jnp.where(
        side == 0,
        jnp.concatenate([kept, came], axis=1),
        jnp.concatenate([came, kept], axis=1),
    )
    other_rows = lax.ppermute(own_rows, "c", SWAP)

    def keep_cols(grid_row):
        marks = lax.dynamic_slice(block_mask, (grid_row * block_rows + side, 0), (1, cols))
        marks = marks.reshape(cols // deep, deep)
        marks = lax.dynamic_slice(marks, (0, lax.axis_index(DEPTH)), (cols // deep, 1))
        return jnp.repeat(marks.reshape(cols // deep).astype(jnp.float32), col_span)

    def by_depth(rows, grid_row):
        rows = rows * keep_cols(grid_row)[None, :]
        return rows.reshape(far, near, row_count, 2 * col_span)

    pieces = jnp.stack(
        [by_depth(own_rows, prow_index), by_depth(other_rows, prow_index ^ 1)], axis=2
    )
    leave = jnp.where(odd == 0, pieces[:, 1], pieces[:, 0]).reshape(-1, 2 * col_span)
    stay = jnp.where(odd == 0, pieces[:, 0], pieces[:, 1]).reshape(-1, 2 * col_span)

    halves = moved.reshape(row_count, CS, half).transpose(1, 0, 2)
    outgoing = jnp.broadcast_to(halves[None], (chunks * YL // CS, CS, row_count, half))
    outgoing = outgoing.reshape(chunks * YL, row_count, half)
    needed = lax.all_to_all(
        outgoing, ALL, 0, 0, tiled=True, axis_index_groups=groups
    ).reshape(2 * col_span, half)

    needed, active_own = lax.optimization_barrier((needed, active_own))
    by_core = active_own.reshape(row_count, 2, half).transpose(1, 0, 2)
    mine = jnp.where(core == 0, by_core[0], by_core[1])
    theirs = jnp.where(core == 0, by_core[1], by_core[0])
    active_pair = jnp.stack([mine, lax.ppermute(theirs, "c", SWAP)])

    here = lax.axis_index(DEPTH)
    keep_here = lax.dynamic_slice(
        active_blocks.reshape(YL, deep, S), (0, here, core * (S // CS)), (YL, 1, S // CS)
    )
    keep_here = jnp.repeat(keep_here, W, axis=2)
    needed = (needed.reshape(YL, col_span, half) * keep_here).reshape(-1, half)

    def product(rows):
        value = jnp.dot(
            rows, needed, precision=lax.Precision.HIGHEST, preferred_element_type=jnp.float32
        )
        return value.reshape(far, 2 * row_count, half)

    leaving = product(leave)
    arrived = lax.ppermute(leaving, "zl", SWAP)
    staying = product(stay)
    staying, arrived = lax.optimization_barrier((staying, arrived))
    pair_sum = staying + arrived
    part = S // 2 * W // lax.axis_size(SIDE)
    own_diag = lax.dynamic_slice_in_dim(
        diag_inverse.reshape(S * W, W), lax.axis_index(BACK) * part, part, 0
    )
    pair_sum, own_diag = lax.optimization_barrier((pair_sum, own_diag))
    parts = lax.all_to_all(pair_sum, "zh", 0, 0, tiled=True)
    summed = jnp.sum(parts, axis=0).reshape(2, row_count, half)

    back = lax.ppermute(summed[1], "c", SWAP)
    full = jnp.where(
        core == 0,
        jnp.concatenate([summed[0], back], axis=1),
        jnp.concatenate([back, summed[0]], axis=1),
    )
    inverse_panels = -(own_keep * full)

    local_diag = jnp.einsum(
        "isa,isb->sab",
        active_pair.reshape(2 * row_count, S // 2, W),
        summed.reshape(2 * row_count, S // 2, W),
        precision=lax.Precision.HIGHEST,
    )
    peers = lax.axis_size(SIDE)
    terms = lax.all_to_all(local_diag.reshape(peers, part, W), SIDE, 0, 0, tiled=True)
    terms = jnp.sum(terms, axis=0)
    terms = own_diag + jnp.sum(spread(terms, "zh"), axis=0)
    diag_blocks = spread(terms, BACK).reshape(S, W, W)
    return (inverse_panels, diag_blocks)


def solution(mesh):
    fine = Mesh(mesh.devices.reshape(YH, XS, CS, YL, ZH, ZL), ALL)
    placed = (P(ROW, COL), P(), P(), P(), P(ALL, None), P())
    return jax.shard_map(
        body,
        mesh=fine,
        in_specs=placed,
        out_specs=(P(ALL, None), P()),
        check_vma=False,
    )
```

```python
import jax
import jax.numpy as jnp
from jax import lax
from jax.sharding import Mesh
from jax.sharding import PartitionSpec as P


BLK = 256
W = 128
S = 4
YH, XS, CS, YL, ZH, ZL = 2, 4, 2, 2, 8, 2
ROW = ("yh", "x", "c")
COL = ("yl", "zh", "zl")
DEPTH = ("zh", "zl")
SIDE = ("yh", "x", "yl", "zl")
BACK = ("c", "yh", "x", "yl", "zl")
ALL = ("yh", "x", "c", "yl", "zh", "zl")
SWAP = [(0, 1), (1, 0)]
FAR_FIRST = [[(ZH // 2 + i) % ZH for i in range(ZH)]]


def flat_of(yh, x, c, yl, zh, zl):
    return ((((yh * XS + x) * CS + c) * YL + yl) * ZH + zh) * ZL + zl


def place_of(flat):
    out = []
    for size in (ZL, ZH, YL, CS, XS, YH):
        out.append(flat % size)
        flat //= size
    return tuple(reversed(out))


def hops(one, two):
    total = 0
    for a, b, size in (
        (one[1], two[1], XS),
        (one[0] * YL + one[3], two[0] * YL + two[3], YH * YL),
        (one[4] * ZL + one[5], two[4] * ZL + two[5], ZH * ZL),
    ):
        gap = abs(a - b) % size
        total += min(gap, size - gap)
    return total


def assign(sources, targets):
    near = [[hops(place_of(s), place_of(t)) for t in targets] for s in sources]
    owner = {}

    def place(s, limit, seen):
        for t in sorted(range(len(targets)), key=lambda t: near[s][t]):
            if near[s][t] > limit or t in seen:
                continue
            seen.add(t)
            if t not in owner or place(owner[t], limit, seen):
                owner[t] = s
                return True
        return False

    limit = 0
    for s in range(len(sources)):
        while not place(s, limit, set()):
            limit += 1
    return {sources[s]: targets[t] for t, s in owner.items()}


def routes(chunks):
    pairs, groups = [], []
    for z in range(ZH * ZL):
        blocks = [h * ZH * ZL + z for h in range(YL)]
        where = {}
        for c in range(CS):
            sources = [q * chunks + j for q in blocks for j in range(c, chunks, CS)]
            targets = [
                flat_of(yh, x, c, yl, z // ZL, z % ZL)
                for yh in range(YH)
                for x in range(XS)
                for yl in range(YL)
            ]
            where.update(assign(sources, targets))
        order = [q * chunks + j for q in blocks for j in range(chunks)]
        pairs += [(source, where[source]) for source in order]
        groups.append([where[source] for source in order])
    return pairs, groups


def spread(value, axis, groups=None):
    copies = jnp.broadcast_to(value[None], (lax.axis_size(axis),) + value.shape)
    return lax.all_to_all(copies, axis, 0, 0, tiled=True, axis_index_groups=groups)


def body(ancestor_inverse, block_mask, block_ids, row_lists, panels, diag_inverse):
    cols = lax.axis_size(COL)
    deep = lax.axis_size(DEPTH)
    far = lax.axis_size("zh")
    near = lax.axis_size("zl")
    prow_index = lax.axis_index(ROW)
    pcol_index = lax.axis_index(COL)
    core = lax.axis_index("c")
    side = lax.axis_index("yl")
    odd = lax.axis_index("zl")
    row_count, width = panels.shape
    half = width // 2
    row_span, col_span = ancestor_inverse.shape
    active_blocks = jnp.any(
        block_ids[:, None, None] == row_lists[None, :, :], axis=2
    ).astype(jnp.float32)
    own_block = (prow_index * cols + pcol_index) * row_count // BLK
    own_active = lax.dynamic_slice_in_dim(active_blocks, own_block, 1, 0)
    own_keep = jnp.repeat(own_active, W, axis=1)
    active_own = panels * own_keep

    chunks = col_span // row_count
    pairs, groups = routes(chunks)

    moved = lax.ppermute(panels, ALL, pairs)

    block_rows = row_span // BLK
    blocks = ancestor_inverse.reshape(block_rows, BLK, col_span)
    kept = jnp.where(side == 0, blocks[0], blocks[1])
    sent = jnp.where(side == 0, blocks[1], blocks[0])
    came = lax.ppermute(sent, "yl", SWAP)
    own_rows = jnp.where(
        side == 0,
        jnp.concatenate([kept, came], axis=1),
        jnp.concatenate([came, kept], axis=1),
    )
    own_rows = lax.optimization_barrier(own_rows)
    other_rows = lax.ppermute(own_rows, "c", SWAP)

    def keep_cols(grid_row):
        marks = lax.dynamic_slice(block_mask, (grid_row * block_rows + side, 0), (1, cols))
        marks = marks.reshape(cols // deep, deep)
        marks = lax.dynamic_slice(marks, (0, lax.axis_index(DEPTH)), (cols // deep, 1))
        return jnp.repeat(marks.reshape(cols // deep).astype(jnp.float32), col_span)

    def by_depth(rows, grid_row):
        rows = rows * keep_cols(grid_row)[None, :]
        rows = rows.reshape(far, near, row_count, 2 * col_span)
        return jnp.roll(rows, -far // 2, axis=0)

    pieces = jnp.stack(
        [by_depth(own_rows, prow_index), by_depth(other_rows, prow_index ^ 1)], axis=2
    )
    leave = jnp.where(odd == 0, pieces[:, 1], pieces[:, 0]).reshape(-1, 2 * col_span)
    stay = jnp.where(odd == 0, pieces[:, 0], pieces[:, 1]).reshape(-1, 2 * col_span)

    halves = moved.reshape(row_count, CS, half).transpose(1, 0, 2)
    outgoing = jnp.broadcast_to(halves[None], (chunks * YL // CS, CS, row_count, half))
    outgoing = outgoing.reshape(chunks * YL, row_count, half)
    needed = lax.all_to_all(
        outgoing, ALL, 0, 0, tiled=True, axis_index_groups=groups
    ).reshape(2 * col_span, half)

    needed, active_own = lax.optimization_barrier((needed, active_own))
    by_core = active_own.reshape(row_count, 2, half).transpose(1, 0, 2)
    mine = jnp.where(core == 0, by_core[0], by_core[1])
    theirs = jnp.where(core == 0, by_core[1], by_core[0])
    active_pair = jnp.stack([mine, lax.ppermute(theirs, "c", SWAP)])

    here = lax.axis_index(DEPTH)
    keep_here = lax.dynamic_slice(
        active_blocks.reshape(YL, deep, S), (0, here, core * (S // CS)), (YL, 1, S // CS)
    )
    keep_here = jnp.repeat(keep_here, W, axis=2)
    needed = (needed.reshape(YL, col_span, half) * keep_here).reshape(-1, half)

    def product(rows):
        value = jnp.dot(
            rows, needed, precision=lax.Precision.HIGHEST, preferred_element_type=jnp.float32
        )
        return value.reshape(far, 2 * row_count, half)

    leaving = product(leave)
    arrived = lax.ppermute(leaving, "zl", SWAP)
    staying = product(stay)
    staying, arrived = lax.optimization_barrier((staying, arrived))
    pair_sum = staying + arrived
    part = S // 2 * W // lax.axis_size(SIDE)
    own_diag = lax.dynamic_slice_in_dim(
        diag_inverse.reshape(S * W, W), lax.axis_index(BACK) * part, part, 0
    )
    pair_sum, own_diag = lax.optimization_barrier((pair_sum, own_diag))
    parts = lax.all_to_all(
        pair_sum, "zh", 0, 0, tiled=True, axis_index_groups=FAR_FIRST
    )
    summed = jnp.sum(parts, axis=0).reshape(2, row_count, half)

    back = lax.ppermute(summed[1], "c", SWAP)
    full = jnp.where(
        core == 0,
        jnp.concatenate([summed[0], back], axis=1),
        jnp.concatenate([back, summed[0]], axis=1),
    )
    inverse_panels = -(own_keep * full)

    local_diag = jnp.einsum(
        "isa,isb->sab",
        active_pair.reshape(2 * row_count, S // 2, W),
        summed.reshape(2 * row_count, S // 2, W),
        precision=lax.Precision.HIGHEST,
    )
    peers = lax.axis_size(SIDE)
    terms = lax.all_to_all(local_diag.reshape(peers, part, W), SIDE, 0, 0, tiled=True)
    terms = jnp.sum(terms, axis=0)
    terms = own_diag + jnp.sum(spread(terms, "zh", FAR_FIRST), axis=0)
    diag_blocks = spread(terms, BACK).reshape(S, W, W)
    return (inverse_panels, diag_blocks)


def solution(mesh):
    fine = Mesh(mesh.devices.reshape(YH, XS, CS, YL, ZH, ZL), ALL)
    placed = (P(ROW, COL), P(), P(), P(), P(ALL, None), P())
    return jax.shard_map(
        body,
        mesh=fine,
        in_specs=placed,
        out_specs=(P(ALL, None), P()),
        check_vma=False,
    )
```

```python
import jax
import jax.numpy as jnp
from jax import lax
from jax.sharding import Mesh
from jax.sharding import PartitionSpec as P


BLK = 256
W = 128
S = 4
YH, XS, CS, YL, ZH, ZL = 2, 4, 2, 2, 8, 2
ROW = ("yh", "x", "c")
COL = ("yl", "zh", "zl")
DEPTH = ("zh", "zl")
SIDE = ("yh", "x", "yl", "zl")
BACK = ("c", "yh", "x", "yl", "zl")
ALL = ("yh", "x", "c", "yl", "zh", "zl")
SWAP = [(0, 1), (1, 0)]
FAR_FIRST = [[(ZH // 2 + i) % ZH for i in range(ZH)]]


def side_order():
    return [
        ((((yh + YH // 2) % YH * XS + (x + XS // 2) % XS) * YL + yl) * ZL) + zl
        for yh in range(YH)
        for x in range(XS)
        for yl in range(YL)
        for zl in range(ZL)
    ]


SIDE_FIRST = [side_order()]
BACK_FIRST = [[c * len(SIDE_FIRST[0]) + m for c in range(CS) for m in SIDE_FIRST[0]]]


def flat_of(yh, x, c, yl, zh, zl):
    return ((((yh * XS + x) * CS + c) * YL + yl) * ZH + zh) * ZL + zl


def place_of(flat):
    out = []
    for size in (ZL, ZH, YL, CS, XS, YH):
        out.append(flat % size)
        flat //= size
    return tuple(reversed(out))


def hops(one, two):
    total = 0
    for a, b, size in (
        (one[1], two[1], XS),
        (one[0] * YL + one[3], two[0] * YL + two[3], YH * YL),
        (one[4] * ZL + one[5], two[4] * ZL + two[5], ZH * ZL),
    ):
        gap = abs(a - b) % size
        total += min(gap, size - gap)
    return total


def assign(sources, targets):
    near = [[hops(place_of(s), place_of(t)) for t in targets] for s in sources]
    owner = {}

    def place(s, limit, seen):
        for t in sorted(range(len(targets)), key=lambda t: near[s][t]):
            if near[s][t] > limit or t in seen:
                continue
            seen.add(t)
            if t not in owner or place(owner[t], limit, seen):
                owner[t] = s
                return True
        return False

    limit = 0
    for s in range(len(sources)):
        while not place(s, limit, set()):
            limit += 1
    return {sources[s]: targets[t] for t, s in owner.items()}


def routes(chunks):
    pairs, groups = [], []
    for z in range(ZH * ZL):
        blocks = [h * ZH * ZL + z for h in range(YL)]
        where = {}
        for c in range(CS):
            sources = [q * chunks + j for q in blocks for j in range(c, chunks, CS)]
            targets = [
                flat_of(yh, x, c, yl, z // ZL, z % ZL)
                for yh in range(YH)
                for x in range(XS)
                for yl in range(YL)
            ]
            where.update(assign(sources, targets))
        order = [q * chunks + j for q in blocks for j in range(chunks)]
        pairs += [(source, where[source]) for source in order]
        groups.append([where[source] for source in order])
    return pairs, groups


def spread(value, axis, groups=None):
    copies = jnp.broadcast_to(value[None], (lax.axis_size(axis),) + value.shape)
    return lax.all_to_all(copies, axis, 0, 0, tiled=True, axis_index_groups=groups)


def body(ancestor_inverse, block_mask, block_ids, row_lists, panels, diag_inverse):
    cols = lax.axis_size(COL)
    deep = lax.axis_size(DEPTH)
    far = lax.axis_size("zh")
    near = lax.axis_size("zl")
    prow_index = lax.axis_index(ROW)
    pcol_index = lax.axis_index(COL)
    core = lax.axis_index("c")
    side = lax.axis_index("yl")
    odd = lax.axis_index("zl")
    row_count, width = panels.shape
    half = width // 2
    row_span, col_span = ancestor_inverse.shape
    active_blocks = jnp.any(
        block_ids[:, None, None] == row_lists[None, :, :], axis=2
    ).astype(jnp.float32)
    own_block = (prow_index * cols + pcol_index) * row_count // BLK
    own_active = lax.dynamic_slice_in_dim(active_blocks, own_block, 1, 0)
    own_keep = jnp.repeat(own_active, W, axis=1)
    active_own = panels * own_keep

    chunks = col_span // row_count
    pairs, groups = routes(chunks)

    moved = lax.ppermute(panels, ALL, pairs)

    block_rows = row_span // BLK
    blocks = ancestor_inverse.reshape(block_rows, BLK, col_span)
    kept = jnp.where(side == 0, blocks[0], blocks[1])
    sent = jnp.where(side == 0, blocks[1], blocks[0])
    came = lax.ppermute(sent, "yl", SWAP)
    own_rows = jnp.where(
        side == 0,
        jnp.concatenate([kept, came], axis=1),
        jnp.concatenate([came, kept], axis=1),
    )
    own_rows = lax.optimization_barrier(own_rows)
    other_rows = lax.ppermute(own_rows, "c", SWAP)

    def keep_cols(grid_row):
        marks = lax.dynamic_slice(block_mask, (grid_row * block_rows + side, 0), (1, cols))
        marks = marks.reshape(cols // deep, deep)
        marks = lax.dynamic_slice(marks, (0, lax.axis_index(DEPTH)), (cols // deep, 1))
        return jnp.repeat(marks.reshape(cols // deep).astype(jnp.float32), col_span)

    def by_depth(rows, grid_row):
        rows = rows * keep_cols(grid_row)[None, :]
        rows = rows.reshape(far, near, row_count, 2 * col_span)
        return jnp.roll(rows, -far // 2, axis=0)

    pieces = jnp.stack(
        [by_depth(own_rows, prow_index), by_depth(other_rows, prow_index ^ 1)], axis=2
    )
    leave = jnp.where(odd == 0, pieces[:, 1], pieces[:, 0]).reshape(-1, 2 * col_span)
    stay = jnp.where(odd == 0, pieces[:, 0], pieces[:, 1]).reshape(-1, 2 * col_span)

    halves = moved.reshape(row_count, CS, half).transpose(1, 0, 2)
    outgoing = jnp.broadcast_to(halves[None], (chunks * YL // CS, CS, row_count, half))
    outgoing = outgoing.reshape(chunks * YL, row_count, half)
    needed = lax.all_to_all(
        outgoing, ALL, 0, 0, tiled=True, axis_index_groups=groups
    ).reshape(2 * col_span, half)

    needed, active_own = lax.optimization_barrier((needed, active_own))
    by_core = active_own.reshape(row_count, 2, half).transpose(1, 0, 2)
    mine = jnp.where(core == 0, by_core[0], by_core[1])
    theirs = jnp.where(core == 0, by_core[1], by_core[0])
    active_pair = jnp.stack([mine, lax.ppermute(theirs, "c", SWAP)])

    here = lax.axis_index(DEPTH)
    keep_here = lax.dynamic_slice(
        active_blocks.reshape(YL, deep, S), (0, here, core * (S // CS)), (YL, 1, S // CS)
    )
    keep_here = jnp.repeat(keep_here, W, axis=2)
    needed = (needed.reshape(YL, col_span, half) * keep_here).reshape(-1, half)

    def product(rows):
        value = jnp.dot(
            rows, needed, precision=lax.Precision.HIGHEST, preferred_element_type=jnp.float32
        )
        return value.reshape(far, 2 * row_count, half)

    leaving = product(leave)
    arrived = lax.ppermute(leaving, "zl", SWAP)
    staying = product(stay)
    staying, arrived = lax.optimization_barrier((staying, arrived))
    pair_sum = staying + arrived
    part = S // 2 * W // lax.axis_size(SIDE)
    far_yh = (lax.axis_index("yh") + YH // 2) % YH
    far_x = (lax.axis_index("x") + XS // 2) % XS
    place = (((core * YH + far_yh) * XS + far_x) * YL + side) * ZL + odd
    own_diag = lax.dynamic_slice_in_dim(diag_inverse.reshape(S * W, W), place * part, part, 0)
    pair_sum, own_diag = lax.optimization_barrier((pair_sum, own_diag))
    parts = lax.all_to_all(
        pair_sum, "zh", 0, 0, tiled=True, axis_index_groups=FAR_FIRST
    )
    summed = jnp.sum(parts, axis=0).reshape(2, row_count, half)

    back = lax.ppermute(summed[1], "c", SWAP)
    full = jnp.where(
        core == 0,
        jnp.concatenate([summed[0], back], axis=1),
        jnp.concatenate([back, summed[0]], axis=1),
    )
    inverse_panels = -(own_keep * full)

    local_diag = jnp.einsum(
        "isa,isb->sab",
        active_pair.reshape(2 * row_count, S // 2, W),
        summed.reshape(2 * row_count, S // 2, W),
        precision=lax.Precision.HIGHEST,
    )
    peers = lax.axis_size(SIDE)
    terms = lax.all_to_all(
        local_diag.reshape(peers, part, W), SIDE, 0, 0, tiled=True, axis_index_groups=SIDE_FIRST
    )
    terms = jnp.sum(terms, axis=0)
    terms = own_diag + jnp.sum(spread(terms, "zh", FAR_FIRST), axis=0)
    diag_blocks = spread(terms, BACK, BACK_FIRST).reshape(S, W, W)
    return (inverse_panels, diag_blocks)


def solution(mesh):
    fine = Mesh(mesh.devices.reshape(YH, XS, CS, YL, ZH, ZL), ALL)
    placed = (P(ROW, COL), P(), P(), P(), P(ALL, None), P())
    return jax.shard_map(
        body,
        mesh=fine,
        in_specs=placed,
        out_specs=(P(ALL, None), P()),
        check_vma=False,
    )
```

```python
import jax
import jax.numpy as jnp
from jax import lax
from jax.sharding import Mesh
from jax.sharding import PartitionSpec as P


BLK = 256
W = 128
S = 4
YH, XS, CS, YL, ZH, ZL = 2, 4, 2, 2, 8, 2
ROW = ("yh", "x", "c")
COL = ("yl", "zh", "zl")
DEPTH = ("zh", "zl")
SIDE = ("yh", "x", "yl", "zl")
BACK = ("c", "yh", "x", "yl", "zl")
ALL = ("yh", "x", "c", "yl", "zh", "zl")
SWAP = [(0, 1), (1, 0)]
FAR_FIRST = [[(ZH // 2 + i) % ZH for i in range(ZH)]]


def side_order():
    return [
        ((((yh + YH // 2) % YH * XS + (x + XS // 2) % XS) * YL + yl) * ZL) + zl
        for yh in range(YH)
        for x in range(XS)
        for yl in range(YL)
        for zl in range(ZL)
    ]


SIDE_FIRST = [side_order()]
BACK_FIRST = [[c * len(SIDE_FIRST[0]) + m for c in range(CS) for m in SIDE_FIRST[0]]]


def flat_of(yh, x, c, yl, zh, zl):
    return ((((yh * XS + x) * CS + c) * YL + yl) * ZH + zh) * ZL + zl


def place_of(flat):
    out = []
    for size in (ZL, ZH, YL, CS, XS, YH):
        out.append(flat % size)
        flat //= size
    return tuple(reversed(out))


def hops(one, two):
    total = 0
    for a, b, size in (
        (one[1], two[1], XS),
        (one[0] * YL + one[3], two[0] * YL + two[3], YH * YL),
        (one[4] * ZL + one[5], two[4] * ZL + two[5], ZH * ZL),
    ):
        gap = abs(a - b) % size
        total += min(gap, size - gap)
    return total


def assign(sources, targets):
    near = [[hops(place_of(s), place_of(t)) for t in targets] for s in sources]
    owner = {}

    def place(s, limit, seen):
        for t in sorted(range(len(targets)), key=lambda t: near[s][t]):
            if near[s][t] > limit or t in seen:
                continue
            seen.add(t)
            if t not in owner or place(owner[t], limit, seen):
                owner[t] = s
                return True
        return False

    limit = 0
    for s in range(len(sources)):
        while not place(s, limit, set()):
            limit += 1
    return {sources[s]: targets[t] for t, s in owner.items()}


def routes(chunks):
    pairs, groups = [], []
    for z in range(ZH * ZL):
        blocks = [h * ZH * ZL + z for h in range(YL)]
        where = {}
        for c in range(CS):
            sources = [q * chunks + j for q in blocks for j in range(c, chunks, CS)]
            targets = [
                flat_of(yh, x, c, yl, z // ZL, z % ZL)
                for yh in range(YH)
                for x in range(XS)
                for yl in range(YL)
            ]
            where.update(assign(sources, targets))
        order = [q * chunks + j for q in blocks for j in range(chunks)]
        pairs += [(source, where[source]) for source in order]
        groups.append([where[source] for source in order])
    return pairs, groups


def spread(value, axis, groups=None):
    copies = jnp.broadcast_to(value[None], (lax.axis_size(axis),) + value.shape)
    return lax.all_to_all(copies, axis, 0, 0, tiled=True, axis_index_groups=groups)


def body(ancestor_inverse, block_mask, block_ids, row_lists, panels, diag_inverse):
    cols = lax.axis_size(COL)
    deep = lax.axis_size(DEPTH)
    far = lax.axis_size("zh")
    near = lax.axis_size("zl")
    prow_index = lax.axis_index(ROW)
    pcol_index = lax.axis_index(COL)
    core = lax.axis_index("c")
    side = lax.axis_index("yl")
    odd = lax.axis_index("zl")
    row_count, width = panels.shape
    half = width // 2
    row_span, col_span = ancestor_inverse.shape
    active_blocks = jnp.any(
        block_ids[:, None, None] == row_lists[None, :, :], axis=2
    ).astype(jnp.float32)
    own_block = (prow_index * cols + pcol_index) * row_count // BLK
    own_active = lax.dynamic_slice_in_dim(active_blocks, own_block, 1, 0)
    own_keep = jnp.repeat(own_active, W, axis=1)
    active_own = panels * own_keep

    chunks = col_span // row_count
    pairs, groups = routes(chunks)

    moved = lax.ppermute(panels, ALL, pairs)

    block_rows = row_span // BLK
    blocks = ancestor_inverse.reshape(block_rows, BLK, col_span)
    kept = jnp.where(side == 0, blocks[0], blocks[1])
    sent = jnp.where(side == 0, blocks[1], blocks[0])
    came = lax.ppermute(sent, "yl", SWAP)
    own_rows = jnp.where(
        side == 0,
        jnp.concatenate([kept, came], axis=1),
        jnp.concatenate([came, kept], axis=1),
    )
    own_rows = lax.optimization_barrier(own_rows)
    other_rows = lax.ppermute(own_rows, "c", SWAP)

    def keep_cols(grid_row):
        marks = lax.dynamic_slice(block_mask, (grid_row * block_rows + side, 0), (1, cols))
        marks = marks.reshape(cols // deep, deep)
        marks = lax.dynamic_slice(marks, (0, lax.axis_index(DEPTH)), (cols // deep, 1))
        return jnp.repeat(marks.reshape(cols // deep).astype(jnp.float32), col_span)

    def by_depth(rows, grid_row):
        rows = rows * keep_cols(grid_row)[None, :]
        rows = rows.reshape(far, near, row_count, 2 * col_span)
        return jnp.roll(rows, -far // 2, axis=0)

    pieces = jnp.stack(
        [by_depth(own_rows, prow_index), by_depth(other_rows, prow_index ^ 1)], axis=2
    )
    leave = jnp.where(odd == 0, pieces[:, 1], pieces[:, 0]).reshape(-1, 2 * col_span)
    stay = jnp.where(odd == 0, pieces[:, 0], pieces[:, 1]).reshape(-1, 2 * col_span)

    halves = jnp.stack([moved[:, :half], moved[:, half:]])
    outgoing = jnp.broadcast_to(halves[None], (chunks * YL // CS, CS, row_count, half))
    outgoing = outgoing.reshape(chunks * YL, row_count, half)
    needed = lax.all_to_all(
        outgoing, ALL, 0, 0, tiled=True, axis_index_groups=groups
    ).reshape(2 * col_span, half)

    needed, active_own = lax.optimization_barrier((needed, active_own))
    by_core = active_own.reshape(row_count, 2, half).transpose(1, 0, 2)
    mine = jnp.where(core == 0, by_core[0], by_core[1])
    theirs = jnp.where(core == 0, by_core[1], by_core[0])
    from_core = lax.ppermute(theirs, "c", SWAP)

    here = lax.axis_index(DEPTH)
    keep_here = lax.dynamic_slice(
        active_blocks.reshape(YL, deep, S), (0, here, core * (S // CS)), (YL, 1, S // CS)
    )
    keep_here = jnp.repeat(keep_here, W, axis=2)
    needed = (needed.reshape(YL, col_span, half) * keep_here).reshape(-1, half)

    def product(rows):
        value = jnp.dot(
            rows, needed, precision=lax.Precision.HIGHEST, preferred_element_type=jnp.float32
        )
        return value.reshape(far, 2 * row_count, half)

    leaving = product(leave)
    arrived = lax.ppermute(leaving, "zl", SWAP)
    staying = product(stay)
    active_pair = jnp.stack([mine, from_core])
    staying, arrived, active_pair = lax.optimization_barrier((staying, arrived, active_pair))
    pair_sum = staying + arrived
    part = S // 2 * W // lax.axis_size(SIDE)
    far_yh = (lax.axis_index("yh") + YH // 2) % YH
    far_x = (lax.axis_index("x") + XS // 2) % XS
    place = (((core * YH + far_yh) * XS + far_x) * YL + side) * ZL + odd
    own_diag = lax.dynamic_slice_in_dim(diag_inverse.reshape(S * W, W), place * part, part, 0)
    pair_sum, own_diag = lax.optimization_barrier((pair_sum, own_diag))
    parts = lax.all_to_all(
        pair_sum, "zh", 0, 0, tiled=True, axis_index_groups=FAR_FIRST
    )
    summed = jnp.sum(parts, axis=0).reshape(2, row_count, half)

    back = lax.ppermute(summed[1], "c", SWAP)
    full = jnp.where(
        core == 0,
        jnp.concatenate([summed[0], back], axis=1),
        jnp.concatenate([back, summed[0]], axis=1),
    )
    inverse_panels = -(own_keep * full)

    local_diag = jnp.einsum(
        "isa,isb->sab",
        active_pair.reshape(2 * row_count, S // 2, W),
        summed.reshape(2 * row_count, S // 2, W),
        precision=lax.Precision.HIGHEST,
    )
    peers = lax.axis_size(SIDE)
    terms = lax.all_to_all(
        local_diag.reshape(peers, part, W), SIDE, 0, 0, tiled=True, axis_index_groups=SIDE_FIRST
    )
    terms = jnp.sum(terms, axis=0)
    terms = own_diag + jnp.sum(spread(terms, "zh", FAR_FIRST), axis=0)
    diag_blocks = spread(terms, BACK, BACK_FIRST).reshape(S, W, W)
    return (inverse_panels, diag_blocks)


def solution(mesh):
    fine = Mesh(mesh.devices.reshape(YH, XS, CS, YL, ZH, ZL), ALL)
    placed = (P(ROW, COL), P(), P(), P(), P(ALL, None), P())
    return jax.shard_map(
        body,
        mesh=fine,
        in_specs=placed,
        out_specs=(P(ALL, None), P()),
        check_vma=False,
    )
```

```python
import jax
import jax.numpy as jnp
from jax import lax
from jax.sharding import Mesh
from jax.sharding import PartitionSpec as P


BLK = 256
W = 128
S = 4
YH, XS, CS, YL, ZH, ZL = 2, 4, 2, 2, 8, 2
ROW = ("yh", "x", "c")
COL = ("yl", "zh", "zl")
DEPTH = ("zh", "zl")
SIDE = ("yh", "x", "yl", "zl")
BACK = ("c", "yh", "x", "yl", "zl")
ALL = ("yh", "x", "c", "yl", "zh", "zl")
SWAP = [(0, 1), (1, 0)]
FAR_FIRST = [[(ZH // 2 + i) % ZH for i in range(ZH)]]


def side_order():
    return [
        ((((yh + YH // 2) % YH * XS + (x + XS // 2) % XS) * YL + yl) * ZL) + zl
        for yh in range(YH)
        for x in range(XS)
        for yl in range(YL)
        for zl in range(ZL)
    ]


SIDE_FIRST = [side_order()]
BACK_FIRST = [[c * len(SIDE_FIRST[0]) + m for c in range(CS) for m in SIDE_FIRST[0]]]


def flat_of(yh, x, c, yl, zh, zl):
    return ((((yh * XS + x) * CS + c) * YL + yl) * ZH + zh) * ZL + zl


def place_of(flat):
    out = []
    for size in (ZL, ZH, YL, CS, XS, YH):
        out.append(flat % size)
        flat //= size
    return tuple(reversed(out))


def hops(one, two):
    total = 0
    for a, b, size in (
        (one[1], two[1], XS),
        (one[0] * YL + one[3], two[0] * YL + two[3], YH * YL),
        (one[4] * ZL + one[5], two[4] * ZL + two[5], ZH * ZL),
    ):
        gap = abs(a - b) % size
        total += min(gap, size - gap)
    return total


def assign(sources, targets):
    near = [[hops(place_of(s), place_of(t)) for t in targets] for s in sources]
    owner = {}

    def place(s, limit, seen):
        for t in sorted(range(len(targets)), key=lambda t: near[s][t]):
            if near[s][t] > limit or t in seen:
                continue
            seen.add(t)
            if t not in owner or place(owner[t], limit, seen):
                owner[t] = s
                return True
        return False

    limit = 0
    for s in range(len(sources)):
        while not place(s, limit, set()):
            limit += 1
    return {sources[s]: targets[t] for t, s in owner.items()}


def routes(chunks):
    pairs, groups = [], []
    for z in range(ZH * ZL):
        blocks = [h * ZH * ZL + z for h in range(YL)]
        where = {}
        for c in range(CS):
            sources = [q * chunks + j for q in blocks for j in range(c, chunks, CS)]
            targets = [
                flat_of(yh, x, c, yl, z // ZL, z % ZL)
                for yh in range(YH)
                for x in range(XS)
                for yl in range(YL)
            ]
            where.update(assign(sources, targets))
        order = [q * chunks + j for q in reversed(blocks) for j in range(chunks)]
        pairs += [(source, where[source]) for source in order]
        groups.append([where[source] for source in order])
    return pairs, groups


def spread(value, axis, groups=None):
    copies = jnp.broadcast_to(value[None], (lax.axis_size(axis),) + value.shape)
    return lax.all_to_all(copies, axis, 0, 0, tiled=True, axis_index_groups=groups)


def body(ancestor_inverse, block_mask, block_ids, row_lists, panels, diag_inverse):
    cols = lax.axis_size(COL)
    deep = lax.axis_size(DEPTH)
    far = lax.axis_size("zh")
    near = lax.axis_size("zl")
    prow_index = lax.axis_index(ROW)
    pcol_index = lax.axis_index(COL)
    core = lax.axis_index("c")
    side = lax.axis_index("yl")
    odd = lax.axis_index("zl")
    row_count, width = panels.shape
    half = width // 2
    row_span, col_span = ancestor_inverse.shape
    active_blocks = jnp.any(
        block_ids[:, None, None] == row_lists[None, :, :], axis=2
    ).astype(jnp.float32)
    own_block = (prow_index * cols + pcol_index) * row_count // BLK
    own_active = lax.dynamic_slice_in_dim(active_blocks, own_block, 1, 0)
    own_keep = jnp.repeat(own_active, W, axis=1)
    active_own = panels * own_keep

    chunks = col_span // row_count
    pairs, groups = routes(chunks)

    moved = lax.ppermute(panels, ALL, pairs)

    block_rows = row_span // BLK
    blocks = ancestor_inverse.reshape(block_rows, BLK, col_span)
    kept = jnp.where(side == 0, blocks[0], blocks[1])
    sent = jnp.where(side == 0, blocks[1], blocks[0])
    came = lax.ppermute(sent, "yl", SWAP)
    own_rows = jnp.where(
        side == 0,
        jnp.concatenate([came, kept], axis=1),
        jnp.concatenate([kept, came], axis=1),
    )
    own_rows = lax.optimization_barrier(own_rows)
    other_rows = lax.ppermute(own_rows, "c", SWAP)

    def keep_cols(grid_row):
        marks = lax.dynamic_slice(block_mask, (grid_row * block_rows + side, 0), (1, cols))
        marks = marks.reshape(cols // deep, deep)
        marks = lax.dynamic_slice(marks, (0, lax.axis_index(DEPTH)), (cols // deep, 1))
        marks = jnp.flip(marks.reshape(cols // deep).astype(jnp.float32))
        return jnp.repeat(marks, col_span)

    def by_depth(rows, grid_row):
        rows = rows * keep_cols(grid_row)[None, :]
        rows = rows.reshape(far, near, row_count, 2 * col_span)
        return jnp.roll(rows, -far // 2, axis=0)

    pieces = jnp.stack(
        [by_depth(own_rows, prow_index), by_depth(other_rows, prow_index ^ 1)], axis=2
    )
    leave = jnp.where(odd == 0, pieces[:, 1], pieces[:, 0]).reshape(-1, 2 * col_span)
    stay = jnp.where(odd == 0, pieces[:, 0], pieces[:, 1]).reshape(-1, 2 * col_span)

    halves = jnp.stack([moved[:, :half], moved[:, half:]])
    outgoing = jnp.broadcast_to(halves[None], (chunks * YL // CS, CS, row_count, half))
    outgoing = outgoing.reshape(chunks * YL, row_count, half)
    needed = lax.all_to_all(
        outgoing, ALL, 0, 0, tiled=True, axis_index_groups=groups
    ).reshape(2 * col_span, half)

    needed, active_own = lax.optimization_barrier((needed, active_own))
    by_core = active_own.reshape(row_count, 2, half).transpose(1, 0, 2)
    mine = jnp.where(core == 0, by_core[0], by_core[1])
    theirs = jnp.where(core == 0, by_core[1], by_core[0])
    from_core = lax.ppermute(theirs, "c", SWAP)

    here = lax.axis_index(DEPTH)
    keep_here = lax.dynamic_slice(
        active_blocks.reshape(YL, deep, S), (0, here, core * (S // CS)), (YL, 1, S // CS)
    )
    keep_here = jnp.repeat(jnp.flip(keep_here, 0), W, axis=2)
    needed = (needed.reshape(YL, col_span, half) * keep_here).reshape(-1, half)

    def product(rows):
        value = jnp.dot(
            rows, needed, precision=lax.Precision.HIGHEST, preferred_element_type=jnp.float32
        )
        return value.reshape(far, 2 * row_count, half)

    leaving = product(leave)
    arrived = lax.ppermute(leaving, "zl", SWAP)
    staying = product(stay)
    active_pair = jnp.stack([mine, from_core])
    staying, arrived, active_pair = lax.optimization_barrier((staying, arrived, active_pair))
    pair_sum = staying + arrived
    part = S // 2 * W // lax.axis_size(SIDE)
    far_yh = (lax.axis_index("yh") + YH // 2) % YH
    far_x = (lax.axis_index("x") + XS // 2) % XS
    place = (((core * YH + far_yh) * XS + far_x) * YL + side) * ZL + odd
    own_diag = lax.dynamic_slice_in_dim(diag_inverse.reshape(S * W, W), place * part, part, 0)
    pair_sum, own_diag = lax.optimization_barrier((pair_sum, own_diag))
    parts = lax.all_to_all(
        pair_sum, "zh", 0, 0, tiled=True, axis_index_groups=FAR_FIRST
    )
    summed = jnp.sum(parts, axis=0).reshape(2, row_count, half)

    back = lax.ppermute(summed[1], "c", SWAP)
    full = jnp.where(
        core == 0,
        jnp.concatenate([summed[0], back], axis=1),
        jnp.concatenate([back, summed[0]], axis=1),
    )
    inverse_panels = -(own_keep * full)

    local_diag = jnp.einsum(
        "isa,isb->sab",
        active_pair.reshape(2 * row_count, S // 2, W),
        summed.reshape(2 * row_count, S // 2, W),
        precision=lax.Precision.HIGHEST,
    )
    peers = lax.axis_size(SIDE)
    terms = lax.all_to_all(
        local_diag.reshape(peers, part, W), SIDE, 0, 0, tiled=True, axis_index_groups=SIDE_FIRST
    )
    terms = jnp.sum(terms, axis=0)
    terms = own_diag + jnp.sum(spread(terms, "zh", FAR_FIRST), axis=0)
    diag_blocks = spread(terms, BACK, BACK_FIRST).reshape(S, W, W)
    return (inverse_panels, diag_blocks)


def solution(mesh):
    fine = Mesh(mesh.devices.reshape(YH, XS, CS, YL, ZH, ZL), ALL)
    placed = (P(ROW, COL), P(), P(), P(), P(ALL, None), P())
    return jax.shard_map(
        body,
        mesh=fine,
        in_specs=placed,
        out_specs=(P(ALL, None), P()),
        check_vma=False,
    )
```
